32 devices in a mesh: snap: 2 (over x), dom: 16 (over z, y, core).
Axes of the slice: x: 2, y: 2, z: 4, core: 2. Of those that a mesh axis runs over, the one named last changes fastest.
Arguments:
- features: bfloat16 [4, 18432, 128], P('snap', 'dom'), may hold values from -6 to 6
- adjacency: bfloat16 [4, 18432, 4, 128], P('snap', 'dom'), may hold values from -0.25 to 0.25
- block_cols: int32 [4, 144, 4], P('snap', 'dom'), may hold values from 0 to 24, as said below
- send_lists: int32 [4, 16, 16], P('snap', 'dom'), may hold values from -1 to 8, as said below
- receive_lists: int32 [4, 16, 16], P('snap', 'dom'), may hold values from -1 to 8, as said below
- spatial_weight: bfloat16 [128, 128], replicated, may hold values from -0.5 to 0.5
- temporal_weight: bfloat16 [3, 128, 256], replicated, may hold values from -0.3125 to 0.3125
- temporal_bias: float32 [256], replicated, may hold values from -3 to 3
- cotangent: bfloat16 [4, 18432, 128], P('snap', 'dom'), may hold values from -6 to 6
Outputs:
- output: bfloat16 [4, 18432, 128], P('snap', 'dom')
- input_grad: bfloat16 [4, 18432, 128], P('snap', 'dom')
The draws below stay inside these ranges and needn't reach their ends.
Inputs may be any that keep to these rules, and one draw needn't show every extreme that they name: receive_lists[s, d, p] is the local index, within partition p, of the one block of 128 items that partition d receives from p in snapshot s, or -1 if none; each partition receives from exactly 15 other partitions and never from itself. send_lists[s, p, d] = receive_lists[s, d, p]: at most one block goes from one partition to another in a snapshot. `block_cols`: for row block r, slot 0 holds r mod 9, its own block; every other slot holds 9 + p for a partition p from which r's partition receives a block in that snapshot, and each such block is named by some slot of the partition.
All inputs are finite; a program needn't handle non-finite values.
Results may differ from the reference program's by a relative error of at most 0.012.
Values may be sent and summed in bfloat16 or wider, within the bound.
No kernel may reach another device: no remote copies, remote signals or barrier semaphores. Data moves between devices by JAX's collectives and lax.ppermute only.
A program may use at most 64 MiB of HBM per device.

```python
import jax
import jax.numpy as jnp
from jax import lax

CHANNELS = 128
BLOCK = 128
SLOTS = 4
TAPS = 3
BLOCKS_DEV = 9
SNAPS = 4
DOMAINS = 16
BLOCKS = 144
ITEMS_DEV = 1152
ITEMS = 18432
HALO = 15


def shuffle_peers(subkey):
    return jax.random.permutation(subkey, DOMAINS - 1)


def boundary_pattern(key):
    base = jax.random.fold_in(key, 4111)
    key_order, key_block, key_extra = jax.random.split(base, 3)
    pair_keys = jax.random.split(key_order, SNAPS * DOMAINS)
    orders = jax.vmap(shuffle_peers)(pair_keys).astype(jnp.int32)
    orders = orders.reshape(SNAPS, DOMAINS, DOMAINS - 1)[:, :, :HALO]
    dom_index = jnp.arange(DOMAINS).astype(jnp.int32)[None, :, None]
    snap_index = jnp.arange(SNAPS).astype(jnp.int32)[:, None, None]
    sources = (dom_index + 1 + orders) % DOMAINS
    chosen = jax.random.randint(key_block, (SNAPS, DOMAINS, HALO), 0, BLOCKS_DEV).astype(jnp.int32)
    receive = jnp.full((SNAPS, DOMAINS, DOMAINS), -1, jnp.int32).at[snap_index, dom_index, sources].set(chosen)
    ref_count = BLOCKS_DEV * (SLOTS - 1)
    position = jnp.arange(ref_count).astype(jnp.int32)[None, None, :]
    spare_slot = jax.random.randint(key_extra, (SNAPS, DOMAINS, ref_count), 0, HALO).astype(jnp.int32)
    halo_slot = jnp.where(position < HALO, position, spare_slot)
    remote_cols = jnp.take_along_axis(sources, halo_slot, axis=2) + BLOCKS_DEV
    remote_cols = remote_cols.reshape(SNAPS, DOMAINS, BLOCKS_DEV, SLOTS - 1)
    own_block = jnp.broadcast_to(jnp.arange(BLOCKS_DEV).astype(jnp.int32)[None, None, :, None], (SNAPS, DOMAINS, BLOCKS_DEV, 1))
    cols = jnp.concatenate([own_block, remote_cols], axis=3).reshape(SNAPS, BLOCKS, SLOTS)
    return (cols.astype(jnp.int32), receive)


def draw_block_cols(key, part):
    return boundary_pattern(key)[0]


def draw_receive_lists(key, part):
    return boundary_pattern(key)[1]


def draw_send_lists(key, part):
    return jnp.transpose(boundary_pattern(key)[1], (0, 2, 1))


def level_of(key, shape, pieces, low, top_value):
    factor_of, own = 1.0, jax.random.fold_in(key, 6)
    for dim, parts in pieces:
        heights = jnp.exp(jax.random.uniform(jax.random.fold_in(own, dim), (parts,), jnp.float32, low / len(pieces), top_value / len(pieces)))
        factor_of = factor_of * jnp.repeat(heights, shape[dim] // parts).reshape([-1 if axis == dim else 1 for axis in range(len(shape))])
    return factor_of


def noise(stream_key, shape, scale, bound, cuts=(), kind=jnp.bfloat16):
    entries = jax.random.normal(stream_key, shape, jnp.float32) * scale
    if len(cuts) > 0:
        entries = level_of(stream_key, shape, cuts, -0.22, 0.18) * entries
    return jnp.clip(entries, min=-bound, max=bound).astype(kind)


def setup_inputs(seed: int = 0) -> dict:
    streams_of = jax.random.split(jax.random.key(seed), 10)
    return {
        "features": noise(streams_of[0], (SNAPS, ITEMS, CHANNELS), 1.0, 6.0, ((0, 2), (1, 16))),
        "adjacency": noise(streams_of[1], (SNAPS, ITEMS, SLOTS, BLOCK), (SLOTS * BLOCK) ** -0.5, 0.25, ((0, 2), (1, 16))),
        "block_cols": draw_block_cols(jax.random.fold_in(streams_of[9], 71), 0),
        "send_lists": draw_send_lists(jax.random.fold_in(streams_of[9], 71), 0),
        "receive_lists": draw_receive_lists(jax.random.fold_in(streams_of[9], 71), 0),
        "spatial_weight": noise(streams_of[5], (CHANNELS, CHANNELS), CHANNELS ** -0.5, 0.5),
        "temporal_weight": noise(streams_of[6], (TAPS, CHANNELS, 2 * CHANNELS), (TAPS * CHANNELS) ** -0.5, 0.3125),
        "temporal_bias": noise(streams_of[7], (2 * CHANNELS,), 0.5, 3.0, (), jnp.float32),
        "cotangent": noise(streams_of[8], (SNAPS, ITEMS, CHANNELS), 1.0, 6.0, ((0, 2), (1, 16))),
    }


def pad_time(values):
    return jnp.pad(values, ((1, 1), (0, 0), (0, 0)))


def temporal_group(operand, temporal_weight, temporal_bias):
    hidden, upstream = operand
    padded = pad_time(hidden).astype(jnp.float32)
    mixture = temporal_bias.astype(jnp.float32)
    for offset in range(TAPS):
        mixture = mixture + jnp.einsum('tic,cd->tid', padded[offset:offset + SNAPS], temporal_weight[offset].astype(jnp.float32))
    linear = mixture[..., :CHANNELS]
    gate_value = jax.nn.sigmoid(mixture[..., CHANNELS:])
    output = (linear * gate_value).astype(jnp.bfloat16)
    upstream_f = upstream.astype(jnp.float32)
    gate_grad = jnp.concatenate([upstream_f * gate_value, upstream_f * linear * gate_value * (1.0 - gate_value)], axis=-1).astype(jnp.bfloat16)
    padded_grad = pad_time(gate_grad).astype(jnp.float32)
    hidden_grad = jnp.zeros(hidden.shape, jnp.float32)
    for offset in range(TAPS):
        start = TAPS - 1 - offset
        hidden_grad = hidden_grad + jnp.einsum('tie,ce->tic', padded_grad[start:start + SNAPS], temporal_weight[offset].astype(jnp.float32))
    return output, hidden_grad.astype(jnp.bfloat16)


def reference(features, adjacency, block_cols, send_lists, receive_lists, spatial_weight, temporal_weight, temporal_bias, cotangent):
    owner = (jnp.arange(BLOCKS) // BLOCKS_DEV).astype(jnp.int32)[None, :, None]
    is_local = block_cols < BLOCKS_DEV
    peer = jnp.clip(block_cols - BLOCKS_DEV, 0, DOMAINS - 1).astype(jnp.int32)
    snap_index = jnp.arange(SNAPS).astype(jnp.int32)[:, None, None]
    remote_block = receive_lists[snap_index, owner, peer]
    global_col = jnp.where(is_local, owner * BLOCKS_DEV + block_cols, peer * BLOCKS_DEV + remote_block).astype(jnp.int32)

    def forward_snapshot(operand):
        feats, tiles_flat, cols = operand
        blocks = feats.reshape(BLOCKS, BLOCK, CHANNELS)
        neighbours = blocks[cols].astype(jnp.float32)
        tiles = tiles_flat.reshape(BLOCKS, BLOCK, SLOTS, BLOCK).astype(jnp.float32)
        aggregated = jnp.einsum('jrkc,jkcd->jrd', tiles, neighbours).astype(jnp.bfloat16).reshape(ITEMS, CHANNELS)
        return jnp.dot(aggregated, spatial_weight, preferred_element_type=jnp.float32).astype(jnp.bfloat16)

    hidden = lax.map(forward_snapshot, (features, adjacency, global_col))

    def by_group(values):
        return values.reshape(SNAPS, DOMAINS, ITEMS_DEV, CHANNELS).transpose(1, 0, 2, 3)

    def ungroup(values):
        return values.transpose(1, 0, 2, 3).reshape(SNAPS, ITEMS, CHANNELS)

    def one_group(operand):
        return temporal_group(operand, temporal_weight, temporal_bias)

    output_groups, grad_groups = lax.map(one_group, (by_group(hidden), by_group(cotangent)))
    output = ungroup(output_groups)
    hidden_grad = ungroup(grad_groups)

    def backward_snapshot(operand):
        tiles_flat, grad_rows, cols, global_cols, sends = operand
        aggregate_grad = jnp.dot(grad_rows, spatial_weight.T, preferred_element_type=jnp.float32).astype(jnp.bfloat16)
        tiles = tiles_flat.reshape(BLOCKS, BLOCK, SLOTS, BLOCK).astype(jnp.float32)
        grad_blocks = aggregate_grad.reshape(BLOCKS, BLOCK, CHANNELS).astype(jnp.float32)
        contribution = jnp.einsum('jrkc,jrd->jkcd', tiles, grad_blocks)
        local_part = jnp.where((cols < BLOCKS_DEV)[:, :, None, None], contribution, 0.0)
        gathered = jnp.zeros((BLOCKS, BLOCK, CHANNELS), jnp.float32)
        gathered = gathered.at[global_cols.reshape(-1)].add(local_part.reshape(BLOCKS * SLOTS, BLOCK, CHANNELS))

        def add_shares(carry, item):
            part, part_cols, send_column = item
            onehot = (part_cols[:, :, None] - BLOCKS_DEV == jnp.arange(DOMAINS).astype(jnp.int32)[None, None, :]).astype(jnp.float32)
            shares = jnp.einsum('jkp,jkcd->pcd', onehot, part, precision=lax.Precision.HIGHEST).astype(jnp.bfloat16)
            shares = lax.optimization_barrier(shares).astype(jnp.float32)
            target = (jnp.arange(DOMAINS).astype(jnp.int32) * BLOCKS_DEV + jnp.maximum(send_column, 0)).astype(jnp.int32)
            return carry.at[target].add(shares), None

        items = (contribution.reshape(DOMAINS, BLOCKS_DEV, SLOTS, BLOCK, CHANNELS), cols.reshape(DOMAINS, BLOCKS_DEV, SLOTS), sends.T)
        gathered, unused = lax.scan(add_shares, gathered, items)
        return gathered.reshape(ITEMS, CHANNELS).astype(jnp.bfloat16)

    input_grad = lax.map(backward_snapshot, (adjacency, hidden_grad, block_cols, global_col, send_lists))
    return output, input_grad
```

```python
import functools

import jax
import jax.numpy as jnp
from jax import lax
from jax.experimental import pallas as pl
from jax.experimental.pallas import tpu as pltpu
from jax.sharding import PartitionSpec as P

F32 = jnp.float32
BF16 = jnp.bfloat16
VMEM = pl.BlockSpec(memory_space=pltpu.VMEM)
SMEM = pl.BlockSpec(memory_space=pltpu.SMEM)
ANY = pl.BlockSpec(memory_space=pl.ANY)
VMEM_LIMIT = 48 * 1024 * 1024


def dot(a, b):
    return jnp.dot(a, b, preferred_element_type=F32)


def shape(dims, dtype=BF16):
    return jax.ShapeDtypeStruct(dims, dtype)


def call(body, outs, in_specs, out_specs, scratch=(), flops=0, moved=0):
    return pl.pallas_call(
        body,
        out_shape=outs,
        in_specs=in_specs,
        out_specs=out_specs,
        scratch_shapes=list(scratch),
        compiler_params=pltpu.CompilerParams(vmem_limit_bytes=VMEM_LIMIT),
        cost_estimate=pl.CostEstimate(flops=flops, bytes_accessed=moved, transcendentals=0),
    )


def inner_index():
    return 1 - lax.axis_index("snap")


def split_index():
    me = lax.axis_index("dom")
    return me // 2, lax.rem(me, 2)


def pack_body(inner, chips, block, send, partner_send, feats, partner_feats, *rest):
    outs, sem = rest[:chips], rest[chips]
    chip, core = split_index()
    snap = inner_index() if inner else 1 - inner_index()
    copies = []
    for offset in range(chips):
        target = 2 * jnp.bitwise_xor(chip, offset) + core
        for which, (lists, source) in enumerate(((send, feats), (partner_send, partner_feats))):
            start = pl.multiple_of(jnp.maximum(lists[snap, 0, target], 0) * block, block)
            copies.append(
                pltpu.make_async_copy(
                    source.at[snap, pl.ds(start, block)],
                    outs[offset].at[which],
                    sem.at[2 * offset + which],
                )
            )
    for copy in copies:
        copy.start()
    for copy in copies:
        copy.wait()


def prep_body(slots, adj, tw, sw, rows_out, cols_out, twt, swt, wide):
    block = adj.shape[2]

    @pl.when(pl.program_id(0) == 0)
    def _():
        for tap in range(tw.shape[0]):
            twt[tap] = tw[tap].astype(F32).T.astype(BF16)
        swt[...] = sw[...].astype(F32).T.astype(BF16)

    wide[...] = adj[0].astype(F32)
    for slot in range(slots):
        tile = wide[pl.ds(slot, block, stride=slots), :]
        rows_out[0, 0, :, slot * block : (slot + 1) * block] = tile.astype(BF16)
        cols_out[0, 0, slot * block : (slot + 1) * block, :] = tile.T.astype(BF16)


def position(column, blocks_here):
    chip, core = split_index()
    part = jnp.clip(column - blocks_here, 0, lax.axis_size("dom") - 1)
    return 2 * jnp.bitwise_xor(part // 2, chip) + jnp.bitwise_xor(lax.rem(part, 2), core)


def hidden_body(inner, chips, blocks_here, slots, cols, feats, tiles, sw, *rest):
    arrived = rest[:chips]
    hidden, own, adj, halo, sem = rest[chips:]
    snap = inner_index() if inner else 1 - inner_index()
    copies = [
        pltpu.make_async_copy(feats.at[snap], own, sem.at[chips]),
        pltpu.make_async_copy(tiles.at[snap], adj, sem.at[chips + 1]),
    ]
    for offset in range(chips):
        copies.append(
            pltpu.make_async_copy(arrived[offset], halo.at[pl.ds(2 * offset, 2)], sem.at[offset])
        )
    for copy in copies:
        copy.start()
    for copy in copies:
        copy.wait()
    block = halo.shape[1]
    for j in range(blocks_here):
        pieces = [own[j * block : (j + 1) * block, :]]
        for slot in range(1, slots):
            pieces.append(halo[position(cols[snap, j, slot], blocks_here)])
        total = dot(adj[j], jnp.concatenate(pieces, axis=0))
        hidden[j * block : (j + 1) * block, :] = dot(total.astype(BF16), sw[...]).astype(BF16)


def spread(snap, j, grad, cols, tiles_t, swt, local, acc, blocks_here, slots):
    block = grad.shape[0]
    agg = dot(grad, swt[...]).astype(BF16)
    parts = dot(tiles_t[j], agg)
    local[j * block : (j + 1) * block, :] = parts[:block]
    for slot in range(1, slots):
        at = position(cols[snap, j, slot], blocks_here)
        acc[at] = acc[at] + parts[slot * block : (slot + 1) * block]


def temporal_body(
    chips, blocks_here, slots, cols, ha, hb, hn, cot, tw, twt, bias, swt, tiles_t, *rest
):
    shares = rest[:chips]
    out, partial, rest_a, local, acc, adj, sem = rest[chips:]
    ia = inner_index()
    ib = 1 - ia
    fetch = pltpu.make_async_copy(tiles_t.at[ib], adj, sem)
    fetch.start()
    flip = lax.axis_index("snap")
    lo, hi = 2 * flip, 2 - 2 * flip
    channels = ha.shape[1]
    block = acc.shape[1]
    acc[...] = jnp.zeros_like(acc)
    fetch.wait()
    for j in range(blocks_here):
        rows = pl.ds(j * block, block)
        xa, xb, xn = ha[rows, :], hb[rows, :], hn[rows, :]
        mix_a = bias[...] + dot(xb, tw[lo]) + dot(xa, tw[1]) + dot(xn, tw[hi])
        mix_b = bias[...] + dot(xb, tw[1]) + dot(xa, tw[hi])
        grads = []
        for index, mix in ((ia, mix_a), (ib, mix_b)):
            linear = mix[:, :channels]
            gate = jax.nn.sigmoid(mix[:, channels:])
            out[index, rows, :] = (linear * gate).astype(BF16)
            up = cot[index, rows, :].astype(F32)
            first = (up * gate).astype(BF16)
            second = (up * linear * gate * (1.0 - gate)).astype(BF16)
            grads.append(jnp.concatenate([first, second], axis=1))
        ga, gb = grads
        partial[rows, :] = dot(ga, twt[hi]).astype(BF16)
        rest_a[rows, :] = dot(ga, twt[1]) + dot(gb, twt[hi])
        grad_b = (dot(ga, twt[lo]) + dot(gb, twt[1])).astype(BF16)
        spread(ib, j, grad_b, cols, adj, swt, local, acc, blocks_here, slots)
    for offset in range(chips):
        shares[offset][...] = acc[2 * offset : 2 * offset + 2].astype(BF16)


def inner_body(chips, blocks_here, slots, cols, rest_a, partial, swt, tiles_t, *rest):
    shares = rest[:chips]
    local, acc, adj, sem = rest[chips:]
    ia = inner_index()
    fetch = pltpu.make_async_copy(tiles_t.at[ia], adj, sem)
    fetch.start()
    block = acc.shape[1]
    acc[...] = jnp.zeros_like(acc)
    fetch.wait()
    for j in range(blocks_here):
        rows = pl.ds(j * block, block)
        grad = (rest_a[rows, :] + partial[rows, :].astype(F32)).astype(BF16)
        spread(ia, j, grad, cols, adj, swt, local, acc, blocks_here, slots)
    for offset in range(chips):
        shares[offset][...] = acc[2 * offset : 2 * offset + 2].astype(BF16)


def collect_body(chips, *refs):
    sources, out, sem = refs[:chips], refs[chips], refs[chips + 1]
    copies = [
        pltpu.make_async_copy(sources[offset].at[1], out.at[offset], sem.at[offset])
        for offset in range(chips)
    ]
    for copy in copies:
        copy.start()
    for copy in copies:
        copy.wait()


def final_body(chips, send, local_a, local_b, swap_a, swap_b, *rest):
    back_a, back_b = rest[:chips], rest[chips : 2 * chips]
    out, acc = rest[2 * chips :]
    chip, core = split_index()
    blocks_here, block = acc.shape[0], acc.shape[1]
    ia = inner_index()
    for snap, local, back, swap in (
        (ia, local_a, back_a, swap_a),
        (1 - ia, local_b, back_b, swap_b),
    ):
        for n in range(blocks_here):
            acc[n] = local[n * block : (n + 1) * block, :]
        for offset in range(chips):
            base = 2 * jnp.bitwise_xor(chip, offset)
            for which in range(2):
                if offset == 0 and which == 0:
                    continue
                source = base + jnp.bitwise_xor(core, which)
                at = send[snap, 0, source]
                value = back[offset][0] if which == 0 else swap[offset]

                @pl.when(at >= 0)
                def _():
                    acc[at] = acc[at] + value.astype(F32)

        for n in range(blocks_here):
            out[snap, n * block : (n + 1) * block, :] = acc[n].astype(BF16)


def local_pair(
    features,
    adjacency,
    block_cols,
    send_lists,
    receive_lists,
    spatial_weight,
    temporal_weight,
    temporal_bias,
    cotangent,
):
    domains = lax.axis_size("dom")
    chips = domains // 2
    snaps_here, items_here, channels = features.shape
    slots, block = adjacency.shape[2:]
    blocks_here = items_here // block
    taps, _, doubled = temporal_weight.shape
    flip_core = [(i, i ^ 1) for i in range(domains)]
    other_snap = [(0, 1), (1, 0)]

    def to_chip(values, offset):
        return lax.ppermute(values, "dom", [(i, i ^ (2 * offset)) for i in range(domains)])

    partner_send = lax.ppermute(send_lists, "dom", flip_core)
    partner_feats = lax.ppermute(features, "dom", flip_core)

    pair = shape((2, block, channels))

    def pack(inner):
        return call(
            functools.partial(pack_body, inner, chips, block),
            [pair] * chips,
            [SMEM, SMEM, ANY, ANY],
            [ANY] * chips,
            [pltpu.SemaphoreType.DMA((2 * chips,))],
            moved=4 * chips * block * channels * 2,
        )(send_lists, partner_send, features, partner_feats)

    def exchange(payload):
        order = sorted(range(1, chips), key=lambda o: -o)
        got = {0: payload[0]}
        for offset in order:
            got[offset] = to_chip(payload[offset], offset)
        return [got[o] for o in range(chips)]

    adj_flat = adjacency.reshape(snaps_here, items_here * slots, block)
    steps = snaps_here * blocks_here
    tile_rows = block * slots
    tiles, tiles_t, twt, swt = pl.pallas_call(
        functools.partial(prep_body, slots),
        grid=(steps,),
        in_specs=[
            pl.BlockSpec((1, tile_rows, block), lambda i: (i // blocks_here, i % blocks_here, 0)),
            pl.BlockSpec((taps, channels, doubled), lambda i: (0, 0, 0)),
            pl.BlockSpec((channels, channels), lambda i: (0, 0)),
        ],
        out_specs=[
            pl.BlockSpec(
                (1, 1, block, tile_rows), lambda i: (i // blocks_here, i % blocks_here, 0, 0)
            ),
            pl.BlockSpec(
                (1, 1, tile_rows, block), lambda i: (i // blocks_here, i % blocks_here, 0, 0)
            ),
            pl.BlockSpec((taps, doubled, channels), lambda i: (0, 0, 0)),
            pl.BlockSpec((channels, channels), lambda i: (0, 0)),
        ],
        out_shape=[
            shape((snaps_here, blocks_here, block, tile_rows)),
            shape((snaps_here, blocks_here, tile_rows, block)),
            shape((taps, doubled, channels)),
            shape((channels, channels)),
        ],
        scratch_shapes=[pltpu.VMEM((tile_rows, block), F32)],
        compiler_params=pltpu.CompilerParams(vmem_limit_bytes=VMEM_LIMIT),
        cost_estimate=pl.CostEstimate(
            flops=0, bytes_accessed=3 * adj_flat.size * 2, transcendentals=0
        ),
    )(adj_flat, temporal_weight, spatial_weight)

    arrived_a = exchange(pack(True))
    arrived_b = exchange(pack(False))

    def hidden_of(inner, arrived):
        return call(
            functools.partial(hidden_body, inner, chips, blocks_here, slots),
            shape((items_here, channels)),
            [SMEM, ANY, ANY, VMEM] + [ANY] * chips,
            VMEM,
            [
                pltpu.VMEM((items_here, channels), BF16),
                pltpu.VMEM((blocks_here, block, tile_rows), BF16),
                pltpu.VMEM((domains, block, channels), BF16),
                pltpu.SemaphoreType.DMA((chips + 2,)),
            ],
            flops=2 * items_here * channels * (tile_rows + channels),
            moved=items_here * tile_rows * 2 + 2 * items_here * channels * 2,
        )(block_cols, features, tiles, spatial_weight, *arrived)

    hidden_a = hidden_of(True, arrived_a)
    hidden_n = lax.ppermute(hidden_a, "snap", other_snap)
    hidden_b = hidden_of(False, arrived_b)

    acc_scratch = [
        pltpu.VMEM((domains, block, channels), F32),
        pltpu.VMEM((blocks_here, tile_rows, block), BF16),
        pltpu.SemaphoreType.DMA,
    ]
    results = call(
        functools.partial(temporal_body, chips, blocks_here, slots),
        [pair] * chips
        + [
            shape((snaps_here, items_here, channels)),
            shape((items_here, channels)),
            shape((items_here, channels), F32),
            shape((items_here, channels), F32),
        ],
        [SMEM] + [VMEM] * 8 + [ANY],
        [VMEM] * (chips + 4),
        acc_scratch,
        flops=30 * items_here * channels * channels,
        moved=20 * items_here * channels * 2,
    )(
        block_cols,
        hidden_a,
        hidden_b,
        hidden_n,
        cotangent,
        temporal_weight,
        twt,
        temporal_bias.reshape(1, doubled),
        swt,
        tiles_t,
    )
    shares_b, (output, partial, rest_a, local_b) = results[:chips], results[chips:]
    partial_n = lax.ppermute(partial, "snap", other_snap)
    back_b = exchange(shares_b)

    results = call(
        functools.partial(inner_body, chips, blocks_here, slots),
        [pair] * chips + [shape((items_here, channels), F32)],
        [SMEM] + [VMEM] * 3 + [ANY],
        [VMEM] * (chips + 1),
        acc_scratch,
        flops=10 * items_here * channels * channels,
        moved=12 * items_here * channels * 2,
    )(block_cols, rest_a, partial_n, swt, tiles_t)
    shares_a, local_a = results[:chips], results[chips]
    back_a = exchange(shares_a)

    def swap(back):
        mine = call(
            functools.partial(collect_body, chips),
            shape((chips, block, channels)),
            [ANY] * chips,
            ANY,
            [pltpu.SemaphoreType.DMA((chips,))],
            moved=2 * chips * block * channels * 2,
        )(*back)
        return lax.ppermute(mine, "dom", flip_core)

    input_grad = call(
        functools.partial(final_body, chips),
        shape((snaps_here, items_here, channels)),
        [SMEM] + [VMEM] * (4 + 2 * chips),
        VMEM,
        [pltpu.VMEM((blocks_here, block, channels), F32)],
        flops=40 * block * channels,
        moved=12 * items_here * channels * 2,
    )(send_lists, local_a, local_b, swap(back_a), swap(back_b), *back_a, *back_b)
    return output, input_grad


def pad_time(values):
    return jnp.pad(values, ((1, 1), (0, 0), (0, 0)))


def to_items(values):
    return lax.all_to_all(values, "snap", split_axis=1, concat_axis=0, tiled=True)


def to_snaps(values):
    return lax.all_to_all(values, "snap", split_axis=0, concat_axis=1, tiled=True)


def gate_terms(padded, temporal_weight, temporal_bias):
    length = padded.shape[0] - 2
    row_count = padded.shape[1]
    channels = padded.shape[2]
    running = jnp.zeros((length * row_count, temporal_weight.shape[2]), jnp.float32)
    for offset in range(temporal_weight.shape[0]):
        window = padded[offset : offset + length].reshape(length * row_count, channels)
        running = running + jnp.dot(
            window, temporal_weight[offset], preferred_element_type=jnp.float32
        )
    return (running + temporal_bias).reshape(length, row_count, -1)


def gate_forward(mixture, channels):
    linear = mixture[..., :channels]
    gate_value = jax.nn.sigmoid(mixture[..., channels:])
    return ((linear * gate_value).astype(jnp.bfloat16), linear, gate_value)


def gate_backward(upstream, linear, gate_value):
    upstream_f = upstream.astype(jnp.float32)
    return jnp.concatenate(
        [upstream_f * gate_value, upstream_f * linear * gate_value * (1.0 - gate_value)], axis=-1
    ).astype(jnp.bfloat16)


def spread_back(padded_grad, temporal_weight):
    length = padded_grad.shape[0] - 2
    row_count = padded_grad.shape[1]
    doubled = padded_grad.shape[2]
    channels = temporal_weight.shape[1]
    taps_count = temporal_weight.shape[0]
    running = jnp.zeros((length * row_count, channels), jnp.float32)
    for offset in range(taps_count):
        start = taps_count - 1 - offset
        window = padded_grad[start : start + length].reshape(length * row_count, doubled)
        running = running + lax.dot_general(
            window,
            temporal_weight[offset],
            (((1,), (1,)), ((), ())),
            preferred_element_type=jnp.float32,
        )
    return running.reshape(length, row_count, channels).astype(jnp.bfloat16)


def local_any(
    features,
    adjacency,
    block_cols,
    send_lists,
    receive_lists,
    spatial_weight,
    temporal_weight,
    temporal_bias,
    cotangent,
):
    domains = lax.axis_size("dom")
    snaps_here, items_here, channels = features.shape
    slot_count = adjacency.shape[2]
    block_size = adjacency.shape[3]
    blocks_here = items_here // block_size
    frame_size = blocks_here + domains
    own_blocks = features.reshape(snaps_here, blocks_here, block_size, channels)
    adjacency_tiles = adjacency.reshape(snaps_here, blocks_here, block_size, slot_count, block_size)
    wanted = send_lists[:, 0, :]
    selector = (wanted[:, :, None] == jnp.arange(blocks_here)[None, None, :]).astype(jnp.bfloat16)
    outgoing = jnp.einsum(
        "sqn,snbc->sqbc", selector, own_blocks, preferred_element_type=jnp.float32
    ).astype(jnp.bfloat16)
    arrived = lax.all_to_all(outgoing, "dom", split_axis=1, concat_axis=1, tiled=True)
    snap_rows = jnp.arange(snaps_here)[:, None, None]
    extended = jnp.concatenate([own_blocks, arrived], axis=1)
    neighbours = extended[snap_rows, block_cols]
    aggregated = jnp.einsum(
        "sjrkc,sjkcd->sjrd", adjacency_tiles, neighbours, preferred_element_type=jnp.float32
    )
    aggregated = aggregated.astype(jnp.bfloat16).reshape(snaps_here * items_here, channels)
    hidden = jnp.dot(aggregated, spatial_weight, preferred_element_type=jnp.float32).astype(
        jnp.bfloat16
    )
    hidden = hidden.reshape(snaps_here, items_here, channels)
    hidden_items = to_items(hidden)
    mixture = gate_terms(pad_time(hidden_items), temporal_weight, temporal_bias)
    output_items, linear, gate_value = gate_forward(mixture, channels)
    output = to_snaps(output_items)
    gate_grad = gate_backward(to_items(cotangent), linear, gate_value)
    hidden_grad = to_snaps(spread_back(pad_time(gate_grad), temporal_weight))
    aggregate_grad = lax.dot_general(
        hidden_grad.reshape(snaps_here * items_here, channels),
        spatial_weight,
        (((1,), (1,)), ((), ())),
        preferred_element_type=jnp.float32,
    ).astype(jnp.bfloat16)
    aggregate_grad = aggregate_grad.reshape(snaps_here, blocks_here, block_size, channels)
    contribution = jnp.einsum(
        "sjrkc,sjrd->sjkcd", adjacency_tiles, aggregate_grad, preferred_element_type=jnp.float32
    )
    placing = (block_cols[..., None] == jnp.arange(frame_size)[None, None, None, :]).astype(
        jnp.float32
    )
    framed = jnp.einsum(
        "sjkf,sjkcd->sfcd",
        placing,
        contribution,
        precision=lax.Precision.HIGHEST,
        preferred_element_type=jnp.float32,
    )
    returned = lax.all_to_all(
        framed[:, blocks_here:].astype(jnp.bfloat16), "dom", split_axis=1, concat_axis=1, tiled=True
    )
    input_grad = framed[:, :blocks_here] + jnp.einsum(
        "sqn,sqbc->snbc", selector, returned, preferred_element_type=jnp.float32
    )
    return (output, input_grad.reshape(snaps_here, items_here, channels).astype(jnp.bfloat16))


def solution(mesh):
    paired = mesh.shape["snap"] == 2 and mesh.shape["dom"] == 16
    return jax.shard_map(
        local_pair if paired else local_any,
        mesh=mesh,
        in_specs=(
            P("snap", "dom", None),
            P("snap", "dom", None, None),
            P("snap", "dom", None),
            P("snap", "dom", None),
            P("snap", "dom", None),
            P(),
            P(),
            P(),
            P("snap", "dom", None),
        ),
        out_specs=(P("snap", "dom", None), P("snap", "dom", None)),
        check_vma=False,
    )
```

```python
import functools

import jax
import jax.numpy as jnp
from jax import lax
from jax.experimental import pallas as pl
from jax.experimental.pallas import tpu as pltpu
from jax.sharding import PartitionSpec as P

F32 = jnp.float32
BF16 = jnp.bfloat16
VMEM = pl.BlockSpec(memory_space=pltpu.VMEM)
SMEM = pl.BlockSpec(memory_space=pltpu.SMEM)
HBM = pl.BlockSpec(memory_space=pltpu.MemorySpace.HBM)
VMEM_LIMIT = 16 * 1024 * 1024
DMA = pltpu.SemaphoreType.DMA
FORWARD = (1, 2, 3, 4, 5, 6, 7)
BACKWARD = (2, 7, 6, 5, 4, 3, 1)
COST = 100


def dot(a, b):
    return jnp.dot(a, b, preferred_element_type=F32)


def dot_t(a, b):
    return lax.dot_general(a, b, (((1,), (1,)), ((), ())), preferred_element_type=F32)


def shape(dims, dtype=BF16):
    return jax.ShapeDtypeStruct(dims, dtype)


def call(body, outs, in_specs, out_specs, scratch=(), flops=0, moved=0):
    return pl.pallas_call(
        body,
        out_shape=outs,
        in_specs=in_specs,
        out_specs=out_specs,
        scratch_shapes=list(scratch),
        compiler_params=pltpu.CompilerParams(vmem_limit_bytes=VMEM_LIMIT),
        cost_estimate=pl.CostEstimate(flops=COST * flops, bytes_accessed=COST * moved, transcendentals=0),
    )


def inner_index():
    return 1 - lax.axis_index("snap")


def split_index():
    me = lax.axis_index("dom")
    return me // 2, lax.rem(me, 2)


def run_copies(pairs, sem):
    copies = [
        pltpu.make_async_copy(source, target, sem.at[i]) for i, (source, target) in enumerate(pairs)
    ]
    for copy in copies:
        copy.start()
    for copy in copies:
        copy.wait()


def wanted(lists, feats, snap, target, block):
    start = pl.multiple_of(jnp.maximum(lists[snap, 0, target], 0) * block, block)
    return feats.at[snap, pl.ds(start, block)]


def pack_inner_body(domains, block, lists, feats, out, send, sem):
    run_copies([(lists, send)], sem)
    ia = inner_index()
    run_copies([(wanted(send, feats, ia, d, block), out.at[d]) for d in range(domains)], sem)


def pack_outer_body(chips, block, send, partner_send, feats, partner_feats, *rest):
    outs, (lists, sem) = rest[:-2], rest[-2:]
    run_copies([(send, lists.at[0]), (partner_send, lists.at[1])], sem)
    send, partner_send = lists.at[0], lists.at[1]
    chip, core = split_index()
    ib = 1 - inner_index()
    pairs = []
    for offset in range(chips):
        target = 2 * jnp.bitwise_xor(chip, offset) + core
        pairs.append((wanted(send, feats, ib, target, block), outs[offset].at[0]))
        pairs.append((wanted(partner_send, partner_feats, ib, target, block), outs[offset].at[1]))
    run_copies(pairs, sem)


def collect_body(picks, *refs):
    sources, out, sem = refs[:-2], refs[-2], refs[-1]
    run_copies([(sources[i].at[j], out.at[n]) for n, (i, j) in enumerate(picks)], sem)


def prep_body(slots, per_step, adj, tw, sw, rows_out, twt, wide):
    block = adj.shape[2]

    @pl.when(pl.program_id(0) == 0)
    def _():
        for tap in range(tw.shape[0]):
            twt[tap] = tw[tap].astype(F32).T.astype(BF16)

    wide[...] = adj[0].astype(F32)
    for n in range(per_step):
        for slot in range(slots):
            tile = wide[pl.ds(n * slots * block + slot, block, stride=slots), :]
            rows_out[0, n, :, slot * block : (slot + 1) * block] = tile.astype(BF16)


def position(column, chips, blocks_here, plain):
    chip, core = split_index()
    part = jnp.clip(column - blocks_here, 0, 2 * chips - 1)
    if plain:
        return part
    which = jnp.bitwise_xor(lax.rem(part, 2), core)
    return which * chips + jnp.bitwise_xor(part // 2, chip)


def aggregate(plain, snap, chips, blocks_here, slots, cols, own, adj, halo, agg, sw, hidden):
    block = halo.shape[1]
    for j in range(blocks_here):
        rows = slice(j * block, (j + 1) * block)
        pieces = [own[rows, :]]
        for slot in range(1, slots):
            pieces.append(halo[position(cols[snap, slot, j], chips, blocks_here, plain)])
        agg[rows, :] = dot(adj[j], jnp.concatenate(pieces, axis=0)).astype(BF16)
    hidden[...] = dot(agg[...], sw[...]).astype(BF16)


def hidden_inner_body(chips, blocks_here, slots, cols, feats, tiles, sw, arrived, *rest):
    hidden, own, adj, halo, agg, sem = rest
    ia = inner_index()
    run_copies([(feats.at[ia], own), (tiles.at[ia], adj), (arrived, halo)], sem)
    aggregate(True, ia, chips, blocks_here, slots, cols, own, adj, halo, agg, sw, hidden)


def hidden_outer_body(chips, blocks_here, slots, cols, feats, tiles, sw, *rest):
    arrived = rest[:chips]
    hidden, own, adj, halo, agg, sem = rest[chips:]
    ib = 1 - inner_index()
    pairs = [(feats.at[ib], own), (tiles.at[ib], adj)]
    for offset in range(chips):
        for which in range(2):
            pairs.append((arrived[offset].at[which], halo.at[which * chips + offset]))
    run_copies(pairs, sem)
    aggregate(False, ib, chips, blocks_here, slots, cols, own, adj, halo, agg, sw, hidden)


def spread(plain, snap, chips, blocks_here, slots, cols, grad, sw, adj, local, acc):
    block = acc.shape[1]
    agg_t = dot_t(sw[...], grad[...]).astype(BF16)
    acc[...] = jnp.zeros_like(acc)
    for j in range(blocks_here):
        parts = dot(agg_t[:, j * block : (j + 1) * block], adj[j])
        local[j] = parts[:, :block]
        for slot in range(1, slots):
            at = position(cols[snap, slot, j], chips, blocks_here, plain)
            acc[at] = acc[at] + parts[:, slot * block : (slot + 1) * block]


def temporal_body(
    chips, blocks_here, slots, tile, cols, ha, hb, hn, cot, tw, twt, bias, sw, tiles, *rest
):
    shares, out, partial, rest_a, local, grad, acc, adj, sem = rest
    ia = inner_index()
    ib = 1 - ia
    fetch = pltpu.make_async_copy(tiles.at[ib], adj, sem)
    fetch.start()
    flip = lax.axis_index("snap")
    lo, hi = 2 * flip, 2 - 2 * flip
    items, channels = ha.shape
    both = jnp.concatenate(
        [
            jnp.concatenate([tw[lo], tw[1]], axis=0),
            jnp.concatenate([tw[1], tw[hi]], axis=0),
        ],
        axis=1,
    )
    back = jnp.concatenate([twt[hi], twt[1]], axis=1)
    for start in range(0, items, tile):
        rows = slice(start, start + tile)
        pair = jnp.concatenate([hb[rows, :], ha[rows, :]], axis=1)
        mixes = dot(pair, both)
        mix_a = mixes[:, : 2 * channels] + dot(hn[rows, :], tw[hi]) + bias[...]
        mix_b = mixes[:, 2 * channels :] + bias[...]
        grads = []
        for index, mix in ((ia, mix_a), (ib, mix_b)):
            linear = mix[:, :channels]
            gate = jax.nn.sigmoid(mix[:, channels:])
            up = cot[index, rows, :].astype(F32)
            gated = linear * gate
            out[index, rows, :] = gated.astype(BF16)
            first = up * gate
            second = up * gated * (1.0 - gate)
            grads.append(jnp.concatenate([first.astype(BF16), second.astype(BF16)], axis=1))
        ga, gb = grads
        from_a = dot(ga, back)
        from_b = dot(gb, back)
        partial[rows, :] = from_a[:, :channels].astype(BF16)
        rest_a[rows, :] = from_a[:, channels:] + from_b[:, :channels]
        grad[rows, :] = (dot(ga, twt[lo]) + from_b[:, channels:]).astype(BF16)
    fetch.wait()
    spread(True, ib, chips, blocks_here, slots, cols, grad, sw, adj, local, acc)
    shares[...] = acc[...].astype(BF16)


def inner_body(chips, blocks_here, slots, cols, rest_a, partial, sw, tiles, *rest):
    outs = rest[:chips]
    local, grad, acc, adj, sem = rest[chips:]
    ia = inner_index()
    fetch = pltpu.make_async_copy(tiles.at[ia], adj, sem)
    fetch.start()
    grad[...] = (rest_a[...] + partial[...].astype(F32)).astype(BF16)
    fetch.wait()
    spread(False, ia, chips, blocks_here, slots, cols, grad, sw, adj, local, acc)
    for offset in range(chips):
        for which in range(2):
            outs[offset][which] = acc[which * chips + offset].astype(BF16)


def add_shares(snap, send, local, terms, acc):
    acc[...] = local[...]
    for source, value in terms:
        at = send[snap, 0, source]

        @pl.when(at >= 0)
        def _():
            acc[at] = acc[at] + value[...].astype(F32)


def finish_rows(acc, n):
    return acc[n].T.astype(BF16)


def source_of(offset, which):
    chip, core = split_index()
    return 2 * jnp.bitwise_xor(chip, offset) + jnp.bitwise_xor(core, which)


def final_outer_body(domains, send, local, arrived, out, acc):
    terms = [(d, arrived.at[d]) for d in range(domains)]
    add_shares(1 - inner_index(), send, local, terms, acc)
    block = acc.shape[1]
    for n in range(acc.shape[0]):
        out[n * block : (n + 1) * block, :] = finish_rows(acc, n)


def final_inner_body(chips, send, local, *rest):
    arrived, acc = rest[: chips - 1], rest[chips - 1]
    terms = [(source_of(offset, 0), arrived[offset - 1].at[0]) for offset in range(1, chips)]
    add_shares(inner_index(), send, local, terms, acc)


def last_body(chips, send, part, swapped, outer, out, acc, sem):
    ia = inner_index()
    move = pltpu.make_async_copy(outer, out.at[1 - ia], sem.at[0])
    move.start()
    terms = [(source_of(offset, 1), swapped.at[offset]) for offset in range(chips)]
    add_shares(ia, send, part, terms, acc)
    block = acc.shape[1]
    for n in range(acc.shape[0]):
        out[ia, n * block : (n + 1) * block, :] = finish_rows(acc, n)
    move.wait()


def local_pair(
    features,
    adjacency,
    block_cols,
    send_lists,
    receive_lists,
    spatial_weight,
    temporal_weight,
    temporal_bias,
    cotangent,
):
    domains = lax.axis_size("dom")
    chips = domains // 2
    snaps_here, items_here, channels = features.shape
    slots, block = adjacency.shape[2:]
    blocks_here = items_here // block
    taps, _, doubled = temporal_weight.shape
    flip_core = [(i, i ^ 1) for i in range(domains)]
    other_snap = [(0, 1), (1, 0)]
    two = shape((2, block, channels))
    block_bytes = block * channels * 2
    item_flops = 2 * items_here * channels * channels

    def swap_cores(values):
        return lax.ppermute(values, "dom", flip_core)

    def exchange(values):
        return lax.all_to_all(values, "dom", split_axis=0, concat_axis=0, tiled=True)

    def to_chips(payloads, order):
        done = {}
        for offset in order:
            pairs = [(i, i ^ (2 * offset)) for i in range(domains)]
            done[offset] = lax.ppermute(payloads[offset], "dom", pairs)
        return [done[offset] for offset in sorted(done)]

    cols = jnp.swapaxes(block_cols, 1, 2)
    partner_send = swap_cores(send_lists)
    partner_feats = swap_cores(features)

    packed_a = call(
        functools.partial(pack_inner_body, domains, block),
        shape((domains, block, channels)),
        [HBM] * 2,
        HBM,
        [pltpu.SMEM(send_lists.shape, jnp.int32), DMA((domains,))],
        moved=2 * domains * block_bytes,
    )(send_lists, features)
    packed_a, partner_send, partner_feats = lax.optimization_barrier(
        (packed_a, partner_send, partner_feats)
    )
    got_a = exchange(packed_a)
    packed = call(
        functools.partial(pack_outer_body, chips, block),
        [two] * chips,
        [HBM] * 4,
        [HBM] * chips,
        [pltpu.SMEM((2, *send_lists.shape), jnp.int32), DMA((domains,))],
        moved=2 * domains * block_bytes,
    )(send_lists, partner_send, features, partner_feats)
    got_b = [packed[0]] + to_chips(packed, FORWARD)

    per_step = 3 if blocks_here % 3 == 0 else 1
    groups = blocks_here // per_step
    tile_rows = block * slots
    adj_flat = adjacency.reshape(snaps_here, items_here * slots, block)
    tiles, twt = pl.pallas_call(
        functools.partial(prep_body, slots, per_step),
        grid=(snaps_here * groups,),
        in_specs=[
            pl.BlockSpec((1, per_step * tile_rows, block), lambda i: (i // groups, i % groups, 0)),
            pl.BlockSpec((taps, channels, doubled), lambda i: (0, 0, 0)),
            pl.BlockSpec((channels, channels), lambda i: (0, 0)),
        ],
        out_specs=[
            pl.BlockSpec(
                (1, per_step, block, tile_rows), lambda i: (i // groups, i % groups, 0, 0)
            ),
            pl.BlockSpec((taps, doubled, channels), lambda i: (0, 0, 0)),
        ],
        out_shape=[
            shape((snaps_here, blocks_here, block, tile_rows)),
            shape((taps, doubled, channels)),
        ],
        scratch_shapes=[pltpu.VMEM((per_step * tile_rows, block), F32)],
        compiler_params=pltpu.CompilerParams(vmem_limit_bytes=VMEM_LIMIT),
        cost_estimate=pl.CostEstimate(
            flops=0, bytes_accessed=2 * adj_flat.size * 2, transcendentals=0
        ),
    )(adj_flat, temporal_weight, spatial_weight)

    def hidden_of(body, arrived):
        return call(
            functools.partial(body, chips, blocks_here, slots),
            shape((items_here, channels)),
            [SMEM, HBM, HBM, VMEM] + [HBM] * len(arrived),
            VMEM,
            [
                pltpu.VMEM((items_here, channels), BF16),
                pltpu.VMEM((blocks_here, block, tile_rows), BF16),
                pltpu.VMEM((domains, block, channels), BF16),
                pltpu.VMEM((items_here, channels), BF16),
                DMA((domains + 2,)),
            ],
            flops=(slots + 1) * item_flops,
            moved=(slots + 4) * items_here * channels * 2,
        )(cols, features, tiles, spatial_weight, *arrived)

    hidden_a = hidden_of(hidden_inner_body, [got_a])
    hidden_n = lax.ppermute(hidden_a, "snap", other_snap)
    hidden_b = hidden_of(hidden_outer_body, got_b)

    back_scratch = [
        pltpu.VMEM((items_here, channels), BF16),
        pltpu.VMEM((domains, block, channels), F32),
        pltpu.VMEM((blocks_here, block, tile_rows), BF16),
        DMA,
    ]
    local_shape = shape((blocks_here, block, channels), F32)
    shares_b, output, partial, rest_a, local_b = call(
        functools.partial(temporal_body, chips, blocks_here, slots, per_step * block),
        [
            shape((domains, block, channels)),
            shape((snaps_here, items_here, channels)),
            shape((items_here, channels)),
            shape((items_here, channels), F32),
            local_shape,
        ],
        [SMEM] + [VMEM] * 8 + [HBM],
        [VMEM] * 5,
        back_scratch,
        flops=26 * item_flops,
        moved=20 * items_here * channels * 2,
    )(
        cols,
        hidden_a,
        hidden_b,
        hidden_n,
        cotangent,
        temporal_weight,
        twt,
        temporal_bias.reshape(1, doubled),
        spatial_weight,
        tiles,
    )
    partial_n = lax.ppermute(partial, "snap", other_snap)
    back_b = exchange(shares_b)

    results = call(
        functools.partial(inner_body, chips, blocks_here, slots),
        [two] * chips + [local_shape],
        [SMEM] + [VMEM] * 3 + [HBM],
        [VMEM] * (chips + 1),
        back_scratch,
        flops=(slots + 1) * item_flops,
        moved=12 * items_here * channels * 2,
    )(cols, rest_a, partial_n, spatial_weight, tiles)
    shares_a, local_a = results[:chips], results[chips]
    back_a = to_chips(shares_a, BACKWARD)
    swapped = swap_cores(
        call(
            functools.partial(collect_body, [(i, 1) for i in range(chips)]),
            shape((chips, block, channels)),
            [HBM] * chips,
            HBM,
            [DMA((chips,))],
            moved=2 * chips * block_bytes,
        )(shares_a[0], *back_a)
    )

    acc = pltpu.VMEM((blocks_here, block, channels), F32)
    cost = dict(flops=domains * block * channels, moved=8 * items_here * channels * 2)
    grad_b = call(
        functools.partial(final_outer_body, domains),
        shape((items_here, channels)),
        [SMEM] + [VMEM] * 2,
        VMEM,
        [acc],
        **cost,
    )(send_lists, local_b, back_b)
    part = call(
        functools.partial(final_inner_body, chips),
        local_shape,
        [SMEM] + [VMEM] * chips,
        VMEM,
        **cost,
    )(send_lists, local_a, *back_a)
    input_grad = call(
        functools.partial(last_body, chips),
        shape((snaps_here, items_here, channels)),
        [SMEM] + [VMEM] * 3,
        VMEM,
        [acc, DMA((1,))],
        **cost,
    )(send_lists, part, swapped, grad_b)
    return output, input_grad


def pad_time(values):
    return jnp.pad(values, ((1, 1), (0, 0), (0, 0)))


def to_items(values):
    return lax.all_to_all(values, "snap", split_axis=1, concat_axis=0, tiled=True)


def to_snaps(values):
    return lax.all_to_all(values, "snap", split_axis=0, concat_axis=1, tiled=True)


def gate_terms(padded, temporal_weight, temporal_bias):
    length = padded.shape[0] - 2
    row_count = padded.shape[1]
    channels = padded.shape[2]
    running = jnp.zeros((length * row_count, temporal_weight.shape[2]), jnp.float32)
    for offset in range(temporal_weight.shape[0]):
        window = padded[offset : offset + length].reshape(length * row_count, channels)
        running = running + jnp.dot(
            window, temporal_weight[offset], preferred_element_type=jnp.float32
        )
    return (running + temporal_bias).reshape(length, row_count, -1)


def gate_forward(mixture, channels):
    linear = mixture[..., :channels]
    gate_value = jax.nn.sigmoid(mixture[..., channels:])
    return ((linear * gate_value).astype(jnp.bfloat16), linear, gate_value)


def gate_backward(upstream, linear, gate_value):
    upstream_f = upstream.astype(jnp.float32)
    return jnp.concatenate(
        [upstream_f * gate_value, upstream_f * linear * gate_value * (1.0 - gate_value)], axis=-1
    ).astype(jnp.bfloat16)


def spread_back(padded_grad, temporal_weight):
    length = padded_grad.shape[0] - 2
    row_count = padded_grad.shape[1]
    doubled = padded_grad.shape[2]
    channels = temporal_weight.shape[1]
    taps_count = temporal_weight.shape[0]
    running = jnp.zeros((length * row_count, channels), jnp.float32)
    for offset in range(taps_count):
        start = taps_count - 1 - offset
        window = padded_grad[start : start + length].reshape(length * row_count, doubled)
        running = running + lax.dot_general(
            window,
            temporal_weight[offset],
            (((1,), (1,)), ((), ())),
            preferred_element_type=jnp.float32,
        )
    return running.reshape(length, row_count, channels).astype(jnp.bfloat16)


def local_any(
    features,
    adjacency,
    block_cols,
    send_lists,
    receive_lists,
    spatial_weight,
    temporal_weight,
    temporal_bias,
    cotangent,
):
    domains = lax.axis_size("dom")
    snaps_here, items_here, channels = features.shape
    slot_count = adjacency.shape[2]
    block_size = adjacency.shape[3]
    blocks_here = items_here // block_size
    frame_size = blocks_here + domains
    own_blocks = features.reshape(snaps_here, blocks_here, block_size, channels)
    adjacency_tiles = adjacency.reshape(snaps_here, blocks_here, block_size, slot_count, block_size)
    wanted = send_lists[:, 0, :]
    selector = (wanted[:, :, None] == jnp.arange(blocks_here)[None, None, :]).astype(jnp.bfloat16)
    outgoing = jnp.einsum(
        "sqn,snbc->sqbc", selector, own_blocks, preferred_element_type=jnp.float32
    ).astype(jnp.bfloat16)
    arrived = lax.all_to_all(outgoing, "dom", split_axis=1, concat_axis=1, tiled=True)
    snap_rows = jnp.arange(snaps_here)[:, None, None]
    extended = jnp.concatenate([own_blocks, arrived], axis=1)
    neighbours = extended[snap_rows, block_cols]
    aggregated = jnp.einsum(
        "sjrkc,sjkcd->sjrd", adjacency_tiles, neighbours, preferred_element_type=jnp.float32
    )
    aggregated = aggregated.astype(jnp.bfloat16).reshape(snaps_here * items_here, channels)
    hidden = jnp.dot(aggregated, spatial_weight, preferred_element_type=jnp.float32).astype(
        jnp.bfloat16
    )
    hidden = hidden.reshape(snaps_here, items_here, channels)
    hidden_items = to_items(hidden)
    mixture = gate_terms(pad_time(hidden_items), temporal_weight, temporal_bias)
    output_items, linear, gate_value = gate_forward(mixture, channels)
    output = to_snaps(output_items)
    gate_grad = gate_backward(to_items(cotangent), linear, gate_value)
    hidden_grad = to_snaps(spread_back(pad_time(gate_grad), temporal_weight))
    aggregate_grad = lax.dot_general(
        hidden_grad.reshape(snaps_here * items_here, channels),
        spatial_weight,
        (((1,), (1,)), ((), ())),
        preferred_element_type=jnp.float32,
    ).astype(jnp.bfloat16)
    aggregate_grad = aggregate_grad.reshape(snaps_here, blocks_here, block_size, channels)
    contribution = jnp.einsum(
        "sjrkc,sjrd->sjkcd", adjacency_tiles, aggregate_grad, preferred_element_type=jnp.float32
    )
    placing = (block_cols[..., None] == jnp.arange(frame_size)[None, None, None, :]).astype(
        jnp.float32
    )
    framed = jnp.einsum(
        "sjkf,sjkcd->sfcd",
        placing,
        contribution,
        precision=lax.Precision.HIGHEST,
        preferred_element_type=jnp.float32,
    )
    returned = lax.all_to_all(
        framed[:, blocks_here:].astype(jnp.bfloat16), "dom", split_axis=1, concat_axis=1, tiled=True
    )
    input_grad = framed[:, :blocks_here] + jnp.einsum(
        "sqn,sqbc->snbc", selector, returned, preferred_element_type=jnp.float32
    )
    return (output, input_grad.reshape(snaps_here, items_here, channels).astype(jnp.bfloat16))


def solution(mesh):
    paired = mesh.shape["snap"] == 2 and mesh.shape["dom"] == 16
    return jax.shard_map(
        local_pair if paired else local_any,
        mesh=mesh,
        in_specs=(
            P("snap", "dom", None),
            P("snap", "dom", None, None),
            P("snap", "dom", None),
            P("snap", "dom", None),
            P("snap", "dom", None),
            P(),
            P(),
            P(),
            P("snap", "dom", None),
        ),
        out_specs=(P("snap", "dom", None), P("snap", "dom", None)),
        check_vma=False,
    )
```

```python
import functools

import jax
import jax.numpy as jnp
from jax import lax
from jax.experimental import pallas as pl
from jax.experimental.pallas import tpu as pltpu
from jax.sharding import PartitionSpec as P

F32 = jnp.float32
BF16 = jnp.bfloat16
VMEM = pl.BlockSpec(memory_space=pltpu.VMEM)
SMEM = pl.BlockSpec(memory_space=pltpu.SMEM)
HBM = pl.BlockSpec(memory_space=pltpu.MemorySpace.HBM)
TILE = 384
VMEM_LIMIT = 16 * 1024 * 1024
DMA = pltpu.SemaphoreType.DMA
FORWARD = (1, 2, 3, 5, 4, 7, 6)
BACKWARD = (1, 2, 3, 5, 4, 7, 6)
COST = 100


def dot(a, b):
    return jnp.dot(a, b, preferred_element_type=F32)


def dot_t(a, b):
    return lax.dot_general(a, b, (((1,), (1,)), ((), ())), preferred_element_type=F32)


def shape(dims, dtype=BF16):
    return jax.ShapeDtypeStruct(dims, dtype)


def shape_hbm(dims, dtype=BF16):
    return pltpu.MemorySpace.HBM(dims, dtype)


def in_hbm(values):
    return pltpu.with_memory_space_constraint(values, pltpu.MemorySpace.HBM)


def call(body, outs, in_specs, out_specs, scratch=(), flops=0, moved=0):
    return pl.pallas_call(
        body,
        out_shape=outs,
        in_specs=in_specs,
        out_specs=out_specs,
        scratch_shapes=list(scratch),
        compiler_params=pltpu.CompilerParams(vmem_limit_bytes=VMEM_LIMIT),
        cost_estimate=pl.CostEstimate(flops=COST * flops, bytes_accessed=COST * moved, transcendentals=0),
    )


def inner_index():
    return 1 - lax.axis_index("snap")


def split_index():
    me = lax.axis_index("dom")
    return me // 2, lax.rem(me, 2)


def run_copies(pairs, sem):
    copies = [
        pltpu.make_async_copy(source, target, sem.at[i]) for i, (source, target) in enumerate(pairs)
    ]
    for copy in copies:
        copy.start()
    for copy in copies:
        copy.wait()


def wanted(lists, feats, snap, target, block):
    start = pl.multiple_of(jnp.maximum(lists[snap, 0, target], 0) * block, block)
    return feats.at[pl.ds(start, block)]


def pack_inner_body(domains, block, lists, feats, out, held, send, sem):
    ia = inner_index()
    run_copies([(lists, send), (feats.at[ia], held)], sem)
    pairs = [(wanted(send, held, ia, d, block), out.at[d]) for d in range(domains)]
    run_copies(pairs, sem)


def pack_outer_body(chips, block, lists, partner_lists, feats, partner_feats, *rest):
    outs, (held, partner_held, send, partner_send, sem) = rest[:-5], rest[-5:]
    chip, core = split_index()
    ib = 1 - inner_index()
    run_copies(
        [
            (lists, send),
            (partner_lists, partner_send),
            (feats.at[ib], held),
            (partner_feats.at[ib], partner_held),
        ],
        sem,
    )
    for offset in range(chips):
        target = 2 * jnp.bitwise_xor(chip, offset) + core
        outs[offset][0] = wanted(send, held, ib, target, block)[...]
        outs[offset][1] = wanted(partner_send, partner_held, ib, target, block)[...]


def collect_body(picks, *refs):
    sources, out, sem = refs[:-2], refs[-2], refs[-1]
    run_copies([(sources[i].at[j], out.at[n]) for n, (i, j) in enumerate(picks)], sem)


def turn_body(tw, twt):
    for tap in range(tw.shape[0]):
        twt[tap] = tw[tap].astype(F32).T.astype(BF16)


def position(column, chips, blocks_here, plain):
    chip, core = split_index()
    part = jnp.clip(column - blocks_here, 0, 2 * chips - 1)
    if plain:
        return part
    which = jnp.bitwise_xor(lax.rem(part, 2), core)
    return which * chips + jnp.bitwise_xor(part // 2, chip)


def side_by_side(snap, slots, adj, wide, tiles):
    blocks_here, block = tiles.shape[:2]
    rows = slots * block
    for j in range(blocks_here):
        wide[j % 2] = adj[snap, j * rows : (j + 1) * rows, :].astype(F32)
        for slot in range(slots):
            tile = wide[j % 2, pl.ds(slot, block, stride=slots), :]
            tiles[j, :, slot * block : (slot + 1) * block] = tile.astype(BF16)


def aggregate(plain, snap, chips, slots, cols, own, tiles, halo, agg, sw, hidden):
    blocks_here, block = tiles.shape[:2]
    for j in range(blocks_here):
        rows = slice(j * block, (j + 1) * block)
        pieces = [own[rows, :]]
        for slot in range(1, slots):
            pieces.append(halo[position(cols[snap, slot, j], chips, blocks_here, plain)])
        agg[rows, :] = dot(tiles[j], jnp.concatenate(pieces, axis=0)).astype(BF16)
    hidden[...] = dot(agg[...], sw[...]).astype(BF16)


def hidden_body(inner, chips, slots, cols, feats, adj, sw, *rest):
    arrived, rest = rest[:-7], rest[-7:]
    hidden, own, wide, tiles, halo, agg, sem = rest
    snap = inner_index() if inner else 1 - inner_index()
    pairs = [(feats.at[snap], own)]
    if inner:
        pairs.append((arrived[0], halo))
    else:
        for offset, source in zip((0,) + FORWARD, arrived):
            for which in range(2):
                pairs.append((source.at[which], halo.at[which * chips + offset]))
    copies = [
        pltpu.make_async_copy(source, target, sem.at[i]) for i, (source, target) in enumerate(pairs)
    ]
    for copy in copies:
        copy.start()
    side_by_side(snap, slots, adj, wide, tiles)
    for copy in copies:
        copy.wait()
    aggregate(inner, snap, chips, slots, cols, own, tiles, halo, agg, sw, hidden)


def spread(plain, snap, chips, blocks_here, slots, cols, grad, sw, adj, local, acc):
    block = acc.shape[1]
    agg_t = dot_t(sw[...], grad[...]).astype(BF16)
    acc[...] = jnp.zeros_like(acc)
    for j in range(blocks_here):
        parts = dot(agg_t[:, j * block : (j + 1) * block], adj[j])
        local[j] = parts[:, :block]
        for slot in range(1, slots):
            at = position(cols[snap, slot, j], chips, blocks_here, plain)
            acc[at] = acc[at] + parts[:, slot * block : (slot + 1) * block]


def temporal_body(
    chips, blocks_here, slots, tile, cols, ha, hb, hn, cot, tw, twt, bias, sw, raw, *rest
):
    shares, out, partial, rest_a, local, grad, acc, adj, wide, sem, held, held_shares = rest
    ia = inner_index()
    ib = 1 - ia
    flip = lax.axis_index("snap")
    lo, hi = 2 * flip, 2 - 2 * flip
    items, channels = ha.shape
    both = jnp.concatenate(
        [
            jnp.concatenate([tw[lo], tw[1]], axis=0),
            jnp.concatenate([tw[1], tw[hi]], axis=0),
        ],
        axis=1,
    )
    back = jnp.concatenate([twt[hi], twt[1]], axis=1)
    for start in range(0, items, tile):
        rows = slice(start, start + tile)
        pair = jnp.concatenate([hb[rows, :], ha[rows, :]], axis=1)
        mixes = dot(pair, both)
        mix_a = mixes[:, : 2 * channels] + dot(hn[rows, :], tw[hi]) + bias[...]
        mix_b = mixes[:, 2 * channels :] + bias[...]
        grads = []
        for index, mix in ((ia, mix_a), (ib, mix_b)):
            linear = mix[:, :channels]
            gate = jax.nn.sigmoid(mix[:, channels:])
            up = cot[index, rows, :].astype(F32)
            gated = linear * gate
            held[index, rows, :] = gated.astype(BF16)
            first = up * gate
            second = up * gated * (1.0 - gate)
            grads.append(jnp.concatenate([first.astype(BF16), second.astype(BF16)], axis=1))
        ga, gb = grads
        from_a = dot(ga, back)
        from_b = dot(gb, back)
        partial[rows, :] = from_a[:, :channels].astype(BF16)
        rest_a[rows, :] = from_a[:, channels:] + from_b[:, :channels]
        grad[rows, :] = (dot(ga, twt[lo]) + from_b[:, channels:]).astype(BF16)
    emit = pltpu.make_async_copy(held, out, sem.at[2])
    emit.start()
    side_by_side(ib, slots, raw, wide, adj)
    spread(True, ib, chips, blocks_here, slots, cols, grad, sw, adj, local, acc)
    half = acc.shape[0] // 2
    copies = [emit]
    for n in range(2):
        some = pl.ds(n * half, half)
        held_shares[some] = acc[some].astype(BF16)
        copies.append(pltpu.make_async_copy(held_shares.at[some], shares.at[some], sem.at[n]))
        copies[-1].start()
    for copy in copies:
        copy.wait()


def inner_body(chips, blocks_here, slots, cols, rest_a, partial, sw, raw, *rest):
    outs = rest[:chips]
    local, grad, acc, adj, wide = rest[chips:]
    ia = inner_index()
    side_by_side(ia, slots, raw, wide, adj)
    grad[...] = (rest_a[...] + partial[...].astype(F32)).astype(BF16)
    spread(False, ia, chips, blocks_here, slots, cols, grad, sw, adj, local, acc)
    for offset in range(chips):
        for which in range(2):
            outs[offset][which] = acc[which * chips + offset].astype(BF16)


def add_shares(snap, send, local, terms, acc):
    acc[...] = local[...]
    for source, value in terms:
        at = send[snap, 0, source]

        @pl.when(at >= 0)
        def _():
            acc[at] = acc[at] + value[...].astype(F32)


def finish_rows(acc, n):
    return acc[n].T.astype(BF16)


def source_of(offset, which):
    chip, core = split_index()
    return 2 * jnp.bitwise_xor(chip, offset) + jnp.bitwise_xor(core, which)


def final_outer_body(domains, send, local, arrived, out, acc):
    terms = [(d, arrived.at[d]) for d in range(domains)]
    add_shares(1 - inner_index(), send, local, terms, acc)
    block = acc.shape[1]
    for n in range(acc.shape[0]):
        out[n * block : (n + 1) * block, :] = finish_rows(acc, n)


def final_inner_body(chips, send, local, *rest):
    arrived, acc = rest[: chips - 1], rest[chips - 1]
    terms = [(source_of(offset, 0), value.at[0]) for offset, value in zip(BACKWARD, arrived)]
    add_shares(inner_index(), send, local, terms, acc)


def last_body(chips, send, part, swapped, outer, out, acc, held, sem):
    ia = inner_index()
    copies = [pltpu.make_async_copy(outer, out.at[1 - ia], sem.at[0])]
    copies[0].start()
    terms = [(source_of(o, 1), swapped.at[n]) for n, o in enumerate((0,) + BACKWARD)]
    add_shares(ia, send, part, terms, acc)
    block = acc.shape[1]
    for n in range(acc.shape[0]):
        rows = pl.ds(n * block, block)
        held[rows, :] = finish_rows(acc, n)
        copies.append(pltpu.make_async_copy(held.at[rows], out.at[ia, rows], sem.at[n + 1]))
        copies[-1].start()
    for copy in copies:
        copy.wait()


def local_pair(
    features,
    adjacency,
    block_cols,
    send_lists,
    receive_lists,
    spatial_weight,
    temporal_weight,
    temporal_bias,
    cotangent,
):
    domains = lax.axis_size("dom")
    chips = domains // 2
    snaps_here, items_here, channels = features.shape
    slots, block = adjacency.shape[2:]
    blocks_here = items_here // block
    taps, _, doubled = temporal_weight.shape
    flip_core = [(i, i ^ 1) for i in range(domains)]
    other_snap = [(0, 1), (1, 0)]
    two = shape((2, block, channels))
    block_bytes = block * channels * 2
    item_flops = 2 * items_here * channels * channels

    def swap_cores(values):
        return lax.ppermute(values, "dom", flip_core)

    def exchange(values):
        return lax.all_to_all(values, "dom", split_axis=0, concat_axis=0, tiled=True)

    def to_chips(payloads, order):
        done = {}
        for offset in order:
            pairs = [(i, i ^ (2 * offset)) for i in range(domains)]
            done[offset] = lax.ppermute(payloads[offset], "dom", pairs)
        return [done[offset] for offset in order]

    cols = jnp.swapaxes(block_cols, 1, 2)
    partner_send = swap_cores(send_lists)
    partner_feats = swap_cores(features)

    packed_a = call(
        functools.partial(pack_inner_body, domains, block),
        shape_hbm((domains, block, channels)),
        [HBM] * 2,
        HBM,
        [
            pltpu.VMEM((items_here, channels), BF16),
            pltpu.SMEM(send_lists.shape, jnp.int32),
            DMA((domains,)),
        ],
        moved=2 * domains * block_bytes,
    )(in_hbm(send_lists), in_hbm(features))
    packed_a, partner_send, partner_feats = lax.optimization_barrier(
        (packed_a, partner_send, partner_feats)
    )
    got_a = exchange(packed_a)
    packed = call(
        functools.partial(pack_outer_body, chips, block),
        [two] * chips,
        [HBM] * 4,
        [VMEM] * chips,
        [
            pltpu.VMEM((items_here, channels), BF16),
            pltpu.VMEM((items_here, channels), BF16),
            pltpu.SMEM(send_lists.shape, jnp.int32),
            pltpu.SMEM(send_lists.shape, jnp.int32),
            DMA((4,)),
        ],
        moved=2 * domains * block_bytes,
    )(*(in_hbm(v) for v in (send_lists, partner_send, features, partner_feats)))
    got_b = [packed[0]] + to_chips(packed, FORWARD)

    tile_rows = block * slots
    adj_flat = adjacency.reshape(snaps_here, items_here * slots, block)
    twt = call(
        turn_body,
        shape((taps, doubled, channels)),
        [VMEM],
        VMEM,
        moved=4 * taps * channels * doubled,
    )(temporal_weight)

    def hidden_of(inner, arrived):
        return call(
            functools.partial(hidden_body, inner, chips, slots),
            shape((items_here, channels)),
            [SMEM, HBM, VMEM, VMEM] + [HBM] * len(arrived),
            VMEM,
            [
                pltpu.VMEM((items_here, channels), BF16),
                pltpu.VMEM((2, tile_rows, block), F32),
                pltpu.VMEM((blocks_here, block, tile_rows), BF16),
                pltpu.VMEM((domains, block, channels), BF16),
                pltpu.VMEM((items_here, channels), BF16),
                DMA((domains + 1,)),
            ],
            flops=(slots + 1) * item_flops,
            moved=(slots + 4) * items_here * channels * 2,
        )(cols, features, adj_flat, spatial_weight, *(in_hbm(v) for v in arrived))

    hidden_a = hidden_of(True, [got_a])
    hidden_n = lax.ppermute(hidden_a, "snap", other_snap)
    hidden_b = hidden_of(False, got_b)

    back_scratch = [
        pltpu.VMEM((items_here, channels), BF16),
        pltpu.VMEM((domains, block, channels), F32),
        pltpu.VMEM((blocks_here, block, tile_rows), BF16),
        pltpu.VMEM((2, tile_rows, block), F32),
    ]
    local_shape = shape((blocks_here, block, channels), F32)
    shares_b, output, partial, rest_a, local_b = call(
        functools.partial(temporal_body, chips, blocks_here, slots, TILE),
        [
            shape_hbm((domains, block, channels)),
            shape_hbm((snaps_here, items_here, channels)),
            shape((items_here, channels)),
            shape((items_here, channels), F32),
            local_shape,
        ],
        [SMEM] + [VMEM] * 9,
        [HBM] * 2 + [VMEM] * 3,
        back_scratch
        + [
            DMA((3,)),
            pltpu.VMEM((snaps_here, items_here, channels), BF16),
            pltpu.VMEM((domains, block, channels), BF16),
        ],
        flops=26 * item_flops,
        moved=20 * items_here * channels * 2,
    )(
        cols,
        hidden_a,
        hidden_b,
        hidden_n,
        cotangent,
        temporal_weight,
        twt,
        temporal_bias.reshape(1, doubled),
        spatial_weight,
        adj_flat,
    )
    partial_n = lax.ppermute(partial, "snap", other_snap)
    back_b = exchange(shares_b)

    results = call(
        functools.partial(inner_body, chips, blocks_here, slots),
        [two] * chips + [local_shape],
        [SMEM] + [VMEM] * 4,
        [VMEM] * (chips + 1),
        back_scratch,
        flops=(slots + 1) * item_flops,
        moved=12 * items_here * channels * 2,
    )(cols, rest_a, partial_n, spatial_weight, adj_flat)
    shares_a, local_a = results[:chips], results[chips]
    back_a = to_chips(shares_a, BACKWARD)
    swapped = swap_cores(
        call(
            functools.partial(collect_body, [(i, 1) for i in range(chips)]),
            shape((chips, block, channels)),
            [HBM] * chips,
            HBM,
            [DMA((chips,))],
            moved=2 * chips * block_bytes,
        )(shares_a[0], *back_a)
    )

    acc = pltpu.VMEM((blocks_here, block, channels), F32)
    cost = dict(flops=domains * block * channels, moved=8 * items_here * channels * 2)
    grad_b = call(
        functools.partial(final_outer_body, domains),
        shape((items_here, channels)),
        [SMEM] + [VMEM] * 2,
        VMEM,
        [acc],
        **cost,
    )(send_lists, local_b, back_b)
    part = call(
        functools.partial(final_inner_body, chips),
        local_shape,
        [SMEM] + [VMEM] * chips,
        VMEM,
        **cost,
    )(send_lists, local_a, *back_a)
    input_grad = call(
        functools.partial(last_body, chips),
        shape_hbm((snaps_here, items_here, channels)),
        [SMEM] + [VMEM] * 3,
        HBM,
        [acc, pltpu.VMEM((items_here, channels), BF16), DMA((blocks_here + 1,))],
        **cost,
    )(send_lists, part, swapped, grad_b)
    return output, input_grad


def pad_time(values):
    return jnp.pad(values, ((1, 1), (0, 0), (0, 0)))


def to_items(values):
    return lax.all_to_all(values, "snap", split_axis=1, concat_axis=0, tiled=True)


def to_snaps(values):
    return lax.all_to_all(values, "snap", split_axis=0, concat_axis=1, tiled=True)


def gate_terms(padded, temporal_weight, temporal_bias):
    length = padded.shape[0] - 2
    row_count = padded.shape[1]
    channels = padded.shape[2]
    running = jnp.zeros((length * row_count, temporal_weight.shape[2]), jnp.float32)
    for offset in range(temporal_weight.shape[0]):
        window = padded[offset : offset + length].reshape(length * row_count, channels)
        running = running + jnp.dot(
            window, temporal_weight[offset], preferred_element_type=jnp.float32
        )
    return (running + temporal_bias).reshape(length, row_count, -1)


def gate_forward(mixture, channels):
    linear = mixture[..., :channels]
    gate_value = jax.nn.sigmoid(mixture[..., channels:])
    return ((linear * gate_value).astype(jnp.bfloat16), linear, gate_value)


def gate_backward(upstream, linear, gate_value):
    upstream_f = upstream.astype(jnp.float32)
    return jnp.concatenate(
        [upstream_f * gate_value, upstream_f * linear * gate_value * (1.0 - gate_value)], axis=-1
    ).astype(jnp.bfloat16)


def spread_back(padded_grad, temporal_weight):
    length = padded_grad.shape[0] - 2
    row_count = padded_grad.shape[1]
    doubled = padded_grad.shape[2]
    channels = temporal_weight.shape[1]
    taps_count = temporal_weight.shape[0]
    running = jnp.zeros((length * row_count, channels), jnp.float32)
    for offset in range(taps_count):
        start = taps_count - 1 - offset
        window = padded_grad[start : start + length].reshape(length * row_count, doubled)
        running = running + lax.dot_general(
            window,
            temporal_weight[offset],
            (((1,), (1,)), ((), ())),
            preferred_element_type=jnp.float32,
        )
    return running.reshape(length, row_count, channels).astype(jnp.bfloat16)


def local_any(
    features,
    adjacency,
    block_cols,
    send_lists,
    receive_lists,
    spatial_weight,
    temporal_weight,
    temporal_bias,
    cotangent,
):
    domains = lax.axis_size("dom")
    snaps_here, items_here, channels = features.shape
    slot_count = adjacency.shape[2]
    block_size = adjacency.shape[3]
    blocks_here = items_here // block_size
    frame_size = blocks_here + domains
    own_blocks = features.reshape(snaps_here, blocks_here, block_size, channels)
    adjacency_tiles = adjacency.reshape(snaps_here, blocks_here, block_size, slot_count, block_size)
    wanted = send_lists[:, 0, :]
    selector = (wanted[:, :, None] == jnp.arange(blocks_here)[None, None, :]).astype(jnp.bfloat16)
    outgoing = jnp.einsum(
        "sqn,snbc->sqbc", selector, own_blocks, preferred_element_type=jnp.float32
    ).astype(jnp.bfloat16)
    arrived = lax.all_to_all(outgoing, "dom", split_axis=1, concat_axis=1, tiled=True)
    snap_rows = jnp.arange(snaps_here)[:, None, None]
    extended = jnp.concatenate([own_blocks, arrived], axis=1)
    neighbours = extended[snap_rows, block_cols]
    aggregated = jnp.einsum(
        "sjrkc,sjkcd->sjrd", adjacency_tiles, neighbours, preferred_element_type=jnp.float32
    )
    aggregated = aggregated.astype(jnp.bfloat16).reshape(snaps_here * items_here, channels)
    hidden = jnp.dot(aggregated, spatial_weight, preferred_element_type=jnp.float32).astype(
        jnp.bfloat16
    )
    hidden = hidden.reshape(snaps_here, items_here, channels)
    hidden_items = to_items(hidden)
    mixture = gate_terms(pad_time(hidden_items), temporal_weight, temporal_bias)
    output_items, linear, gate_value = gate_forward(mixture, channels)
    output = to_snaps(output_items)
    gate_grad = gate_backward(to_items(cotangent), linear, gate_value)
    hidden_grad = to_snaps(spread_back(pad_time(gate_grad), temporal_weight))
    aggregate_grad = lax.dot_general(
        hidden_grad.reshape(snaps_here * items_here, channels),
        spatial_weight,
        (((1,), (1,)), ((), ())),
        preferred_element_type=jnp.float32,
    ).astype(jnp.bfloat16)
    aggregate_grad = aggregate_grad.reshape(snaps_here, blocks_here, block_size, channels)
    contribution = jnp.einsum(
        "sjrkc,sjrd->sjkcd", adjacency_tiles, aggregate_grad, preferred_element_type=jnp.float32
    )
    placing = (block_cols[..., None] == jnp.arange(frame_size)[None, None, None, :]).astype(
        jnp.float32
    )
    framed = jnp.einsum(
        "sjkf,sjkcd->sfcd",
        placing,
        contribution,
        precision=lax.Precision.HIGHEST,
        preferred_element_type=jnp.float32,
    )
    returned = lax.all_to_all(
        framed[:, blocks_here:].astype(jnp.bfloat16), "dom", split_axis=1, concat_axis=1, tiled=True
    )
    input_grad = framed[:, :blocks_here] + jnp.einsum(
        "sqn,sqbc->snbc", selector, returned, preferred_element_type=jnp.float32
    )
    return (output, input_grad.reshape(snaps_here, items_here, channels).astype(jnp.bfloat16))


def solution(mesh):
    paired = mesh.shape["snap"] == 2 and mesh.shape["dom"] == 16
    return jax.shard_map(
        local_pair if paired else local_any,
        mesh=mesh,
        in_specs=(
            P("snap", "dom", None),
            P("snap", "dom", None, None),
            P("snap", "dom", None),
            P("snap", "dom", None),
            P("snap", "dom", None),
            P(),
            P(),
            P(),
            P("snap", "dom", None),
        ),
        out_specs=(P("snap", "dom", None), P("snap", "dom", None)),
        check_vma=False,
    )
```

```python
import functools

import jax
import jax.numpy as jnp
from jax import lax
from jax.experimental import pallas as pl
from jax.experimental.pallas import tpu as pltpu
from jax.sharding import PartitionSpec as P

F32 = jnp.float32
BF16 = jnp.bfloat16
VMEM = pl.BlockSpec(memory_space=pltpu.VMEM)
SMEM = pl.BlockSpec(memory_space=pltpu.SMEM)
HBM = pl.BlockSpec(memory_space=pltpu.MemorySpace.HBM)
TILE = 384
VMEM_LIMIT = 16 * 1024 * 1024
DMA = pltpu.SemaphoreType.DMA
FORWARD = (1, 2, 3, 5, 4, 7, 6)
BACKWARD = (1, 2, 3, 5, 4, 7, 6)
COST = 100


def dot(a, b):
    return jnp.dot(a, b, preferred_element_type=F32)


def dot_t(a, b):
    return lax.dot_general(a, b, (((1,), (1,)), ((), ())), preferred_element_type=F32)


def shape(dims, dtype=BF16):
    return jax.ShapeDtypeStruct(dims, dtype)


def shape_hbm(dims, dtype=BF16):
    return pltpu.MemorySpace.HBM(dims, dtype)


def in_hbm(values):
    return pltpu.with_memory_space_constraint(values, pltpu.MemorySpace.HBM)


def call(body, outs, in_specs, out_specs, scratch=(), flops=0, moved=0):
    return pl.pallas_call(
        body,
        out_shape=outs,
        in_specs=in_specs,
        out_specs=out_specs,
        scratch_shapes=list(scratch),
        compiler_params=pltpu.CompilerParams(vmem_limit_bytes=VMEM_LIMIT),
        cost_estimate=pl.CostEstimate(flops=COST * flops, bytes_accessed=COST * moved, transcendentals=0),
    )


def inner_index():
    return 1 - lax.axis_index("snap")


def split_index():
    me = lax.axis_index("dom")
    return me // 2, lax.rem(me, 2)


def run_copies(pairs, sem):
    copies = [
        pltpu.make_async_copy(source, target, sem.at[i]) for i, (source, target) in enumerate(pairs)
    ]
    for copy in copies:
        copy.start()
    for copy in copies:
        copy.wait()


def wanted(lists, feats, snap, target, block):
    start = pl.multiple_of(jnp.maximum(lists[snap, 0, target], 0) * block, block)
    return feats.at[pl.ds(start, block)]


def pack_inner_body(domains, block, lists, feats, out, held, send, sem):
    ia = inner_index()
    run_copies([(lists, send), (feats.at[ia], held)], sem)
    pairs = [(wanted(send, held, ia, d, block), out.at[d]) for d in range(domains)]
    run_copies(pairs, sem)


def pack_outer_body(chips, block, lists, partner_lists, feats, partner_feats, *rest):
    outs, (held, partner_held, send, partner_send, sem) = rest[:-5], rest[-5:]
    chip, core = split_index()
    ib = 1 - inner_index()
    run_copies(
        [
            (lists, send),
            (partner_lists, partner_send),
            (feats.at[ib], held),
            (partner_feats.at[ib], partner_held),
        ],
        sem,
    )
    for offset in range(chips):
        target = 2 * jnp.bitwise_xor(chip, offset) + core
        outs[offset][0] = wanted(send, held, ib, target, block)[...]
        outs[offset][1] = wanted(partner_send, partner_held, ib, target, block)[...]


def collect_body(picks, *refs):
    sources, out, sem = refs[:-2], refs[-2], refs[-1]
    run_copies([(sources[i].at[j], out.at[n]) for n, (i, j) in enumerate(picks)], sem)


def turn_body(tw, twt):
    for tap in range(tw.shape[0]):
        twt[tap] = tw[tap].astype(F32).T.astype(BF16)


def position(column, chips, blocks_here, plain):
    chip, core = split_index()
    part = jnp.clip(column - blocks_here, 0, 2 * chips - 1)
    if plain:
        return part
    which = jnp.bitwise_xor(lax.rem(part, 2), core)
    return which * chips + jnp.bitwise_xor(part // 2, chip)


def side_by_side(snap, slots, adj, wide, tiles, fetches=()):
    blocks_here, block = tiles.shape[:2]
    rows = slots * block
    for j in range(blocks_here):
        if fetches and j % 3 == 0:
            fetches[j // 3].wait()
        wide[j % 2] = adj[snap, j * rows : (j + 1) * rows, :].astype(F32)
        for slot in range(slots):
            tile = wide[j % 2, pl.ds(slot, block, stride=slots), :]
            tiles[j, :, slot * block : (slot + 1) * block] = tile.astype(BF16)


def aggregate(plain, snap, chips, slots, cols, own, tiles, halo, agg, sw, hidden):
    blocks_here, block = tiles.shape[:2]
    for j in range(blocks_here):
        rows = slice(j * block, (j + 1) * block)
        pieces = [own[rows, :]]
        for slot in range(1, slots):
            pieces.append(halo[position(cols[snap, slot, j], chips, blocks_here, plain)])
        agg[rows, :] = dot(tiles[j], jnp.concatenate(pieces, axis=0)).astype(BF16)
    hidden[...] = dot(agg[...], sw[...]).astype(BF16)


def hidden_body(inner, chips, slots, cols, feats, adj, weight, *rest):
    arrived, rest = rest[:-8], rest[-8:]
    hidden, own, sw, wide, tiles, halo, agg, sem = rest
    snap = inner_index() if inner else 1 - inner_index()
    pairs = [(feats.at[snap], own), (weight, sw)]
    if inner:
        pairs.append((arrived[0], halo))
    else:
        for offset, source in zip((0,) + FORWARD, arrived):
            for which in range(2):
                pairs.append((source.at[which], halo.at[which * chips + offset]))
    copies = [
        pltpu.make_async_copy(source, target, sem.at[i]) for i, (source, target) in enumerate(pairs)
    ]
    for copy in copies:
        copy.start()
    side_by_side(snap, slots, adj, wide, tiles)
    for copy in copies:
        copy.wait()
    aggregate(inner, snap, chips, slots, cols, own, tiles, halo, agg, sw, hidden)


def spread(plain, snap, chips, blocks_here, slots, cols, grad, sw, adj, local, acc):
    block = acc.shape[1]
    agg_t = dot_t(sw[...], grad[...]).astype(BF16)
    acc[...] = jnp.zeros_like(acc)
    for j in range(blocks_here):
        parts = dot(agg_t[:, j * block : (j + 1) * block], adj[j])
        local[j] = parts[:, :block]
        for slot in range(1, slots):
            at = position(cols[snap, slot, j], chips, blocks_here, plain)
            acc[at] = acc[at] + parts[:, slot * block : (slot + 1) * block]


def temporal_body(
    chips, blocks_here, slots, tile, cols, ha, hb, hn, cot, tw, twt, bias, sw, raw, *rest
):
    shares, out, partial, rest_a, local, grad, acc, adj, wide, sem, held, held_shares = rest
    ia = inner_index()
    ib = 1 - ia
    flip = lax.axis_index("snap")
    lo, hi = 2 * flip, 2 - 2 * flip
    items, channels = ha.shape
    both = jnp.concatenate(
        [
            jnp.concatenate([tw[lo], tw[1]], axis=0),
            jnp.concatenate([tw[1], tw[hi]], axis=0),
        ],
        axis=1,
    )
    back = jnp.concatenate([twt[hi], twt[1]], axis=1)
    for start in range(0, items, tile):
        rows = slice(start, start + tile)
        pair = jnp.concatenate([hb[rows, :], ha[rows, :]], axis=1)
        mixes = dot(pair, both)
        mix_a = mixes[:, : 2 * channels] + dot(hn[rows, :], tw[hi]) + bias[...]
        mix_b = mixes[:, 2 * channels :] + bias[...]
        grads = []
        for index, mix in ((ia, mix_a), (ib, mix_b)):
            linear = mix[:, :channels]
            gate = jax.nn.sigmoid(mix[:, channels:])
            up = cot[index, rows, :].astype(F32)
            gated = linear * gate
            held[index, rows, :] = gated.astype(BF16)
            first = up * gate
            second = up * gated * (1.0 - gate)
            grads.append(jnp.concatenate([first.astype(BF16), second.astype(BF16)], axis=1))
        ga, gb = grads
        from_a = dot(ga, back)
        from_b = dot(gb, back)
        partial[rows, :] = from_a[:, :channels].astype(BF16)
        rest_a[rows, :] = from_a[:, channels:] + from_b[:, :channels]
        grad[rows, :] = (dot(ga, twt[lo]) + from_b[:, channels:]).astype(BF16)
    emit = pltpu.make_async_copy(held, out, sem.at[2])
    emit.start()
    side_by_side(ib, slots, raw, wide, adj)
    spread(True, ib, chips, blocks_here, slots, cols, grad, sw, adj, local, acc)
    half = acc.shape[0] // 2
    copies = [emit]
    for n in range(2):
        some = pl.ds(n * half, half)
        held_shares[some] = acc[some].astype(BF16)
        copies.append(pltpu.make_async_copy(held_shares.at[some], shares.at[some], sem.at[n]))
        copies[-1].start()
    for copy in copies:
        copy.wait()


def inner_body(chips, blocks_here, slots, cols, rest_a, partial, sw, raw, *rest):
    outs = rest[:chips]
    local, grad, acc, adj, wide, held, sem = rest[chips:]
    ia = inner_index()
    rows = held.shape[1] // blocks_here
    fetches = []
    for j in range(0, blocks_here, 3):
        some = pl.ds(j * rows, min(3, blocks_here - j) * rows)
        fetches.append(
            pltpu.make_async_copy(raw.at[ia, some], held.at[0, some], sem.at[len(fetches)])
        )
        fetches[-1].start()
    grad[...] = (rest_a[...] + partial[...].astype(F32)).astype(BF16)
    side_by_side(0, slots, held, wide, adj, fetches)
    spread(False, ia, chips, blocks_here, slots, cols, grad, sw, adj, local, acc)
    for offset in range(chips):
        for which in range(2):
            outs[offset][which] = acc[which * chips + offset].astype(BF16)


def add_shares(snap, send, local, terms, acc):
    acc[...] = local[...]
    for source, value in terms:
        at = send[snap, 0, source]

        @pl.when(at >= 0)
        def _():
            acc[at] = acc[at] + value[...].astype(F32)


def finish_rows(acc, n):
    return acc[n].T.astype(BF16)


def source_of(offset, which):
    chip, core = split_index()
    return 2 * jnp.bitwise_xor(chip, offset) + jnp.bitwise_xor(core, which)


def final_outer_body(domains, send, local, arrived, out, acc):
    terms = [(d, arrived.at[d]) for d in range(domains)]
    add_shares(1 - inner_index(), send, local, terms, acc)
    block = acc.shape[1]
    for n in range(acc.shape[0]):
        out[n * block : (n + 1) * block, :] = finish_rows(acc, n)


def final_inner_body(chips, send, local, *rest):
    arrived, acc = rest[: chips - 1], rest[chips - 1]
    terms = [(source_of(offset, 0), value.at[0]) for offset, value in zip(BACKWARD, arrived)]
    add_shares(inner_index(), send, local, terms, acc)


def last_body(chips, send, part, swapped, outer, out, acc, held, sem):
    ia = inner_index()
    copies = [pltpu.make_async_copy(outer, out.at[1 - ia], sem.at[0])]
    copies[0].start()
    terms = [(source_of(o, 1), swapped.at[n]) for n, o in enumerate((0,) + BACKWARD)]
    add_shares(ia, send, part, terms, acc)
    block = acc.shape[1]
    for n in range(acc.shape[0]):
        rows = pl.ds(n * block, block)
        held[rows, :] = finish_rows(acc, n)
        copies.append(pltpu.make_async_copy(held.at[rows], out.at[ia, rows], sem.at[n + 1]))
        copies[-1].start()
    for copy in copies:
        copy.wait()


def local_pair(
    features,
    adjacency,
    block_cols,
    send_lists,
    receive_lists,
    spatial_weight,
    temporal_weight,
    temporal_bias,
    cotangent,
):
    domains = lax.axis_size("dom")
    chips = domains // 2
    snaps_here, items_here, channels = features.shape
    slots, block = adjacency.shape[2:]
    blocks_here = items_here // block
    taps, _, doubled = temporal_weight.shape
    flip_core = [(i, i ^ 1) for i in range(domains)]
    other_snap = [(0, 1), (1, 0)]
    two = shape((2, block, channels))
    block_bytes = block * channels * 2
    item_flops = 2 * items_here * channels * channels

    def swap_cores(values):
        return lax.ppermute(values, "dom", flip_core)

    def exchange(values):
        return lax.all_to_all(values, "dom", split_axis=0, concat_axis=0, tiled=True)

    def to_chips(payloads, order):
        done = {}
        for offset in order:
            pairs = [(i, i ^ (2 * offset)) for i in range(domains)]
            done[offset] = lax.ppermute(payloads[offset], "dom", pairs)
        return [done[offset] for offset in order]

    cols = jnp.swapaxes(block_cols, 1, 2)
    partner_send = swap_cores(send_lists)
    partner_feats = swap_cores(features)

    packed_a = call(
        functools.partial(pack_inner_body, domains, block),
        shape_hbm((domains, block, channels)),
        [HBM] * 2,
        HBM,
        [
            pltpu.VMEM((items_here, channels), BF16),
            pltpu.SMEM(send_lists.shape, jnp.int32),
            DMA((domains,)),
        ],
        moved=2 * domains * block_bytes,
    )(in_hbm(send_lists), in_hbm(features))
    packed_a, partner_send, partner_feats = lax.optimization_barrier(
        (packed_a, partner_send, partner_feats)
    )
    got_a = exchange(packed_a)
    packed = call(
        functools.partial(pack_outer_body, chips, block),
        [two] * chips,
        [HBM] * 4,
        [VMEM] * chips,
        [
            pltpu.VMEM((items_here, channels), BF16),
            pltpu.VMEM((items_here, channels), BF16),
            pltpu.SMEM(send_lists.shape, jnp.int32),
            pltpu.SMEM(send_lists.shape, jnp.int32),
            DMA((4,)),
        ],
        moved=2 * domains * block_bytes,
    )(*(in_hbm(v) for v in (send_lists, partner_send, features, partner_feats)))
    got_b = [packed[0]] + to_chips(packed, FORWARD)

    tile_rows = block * slots
    adj_flat = adjacency.reshape(snaps_here, items_here * slots, block)
    twt = call(
        turn_body,
        shape((taps, doubled, channels)),
        [VMEM],
        VMEM,
        moved=4 * taps * channels * doubled,
    )(temporal_weight)

    def hidden_of(inner, arrived):
        return call(
            functools.partial(hidden_body, inner, chips, slots),
            shape((items_here, channels)),
            [SMEM, HBM, VMEM, HBM] + [HBM] * len(arrived),
            VMEM,
            [
                pltpu.VMEM((items_here, channels), BF16),
                pltpu.VMEM((channels, channels), BF16),
                pltpu.VMEM((2, tile_rows, block), F32),
                pltpu.VMEM((blocks_here, block, tile_rows), BF16),
                pltpu.VMEM((domains, block, channels), BF16),
                pltpu.VMEM((items_here, channels), BF16),
                DMA((domains + 2,)),
            ],
            flops=(slots + 1) * item_flops,
            moved=(slots + 4) * items_here * channels * 2,
        )(cols, features, adj_flat, in_hbm(spatial_weight), *(in_hbm(v) for v in arrived))

    hidden_a = hidden_of(True, [got_a])
    hidden_n = lax.ppermute(hidden_a, "snap", other_snap)
    hidden_b = hidden_of(False, got_b)

    back_scratch = [
        pltpu.VMEM((items_here, channels), BF16),
        pltpu.VMEM((domains, block, channels), F32),
        pltpu.VMEM((blocks_here, block, tile_rows), BF16),
        pltpu.VMEM((2, tile_rows, block), F32),
    ]
    local_shape = shape((blocks_here, block, channels), F32)
    shares_b, output, partial, rest_a, local_b = call(
        functools.partial(temporal_body, chips, blocks_here, slots, TILE),
        [
            shape_hbm((domains, block, channels)),
            shape_hbm((snaps_here, items_here, channels)),
            shape((items_here, channels)),
            shape((items_here, channels), F32),
            local_shape,
        ],
        [SMEM] + [VMEM] * 9,
        [HBM] * 2 + [VMEM] * 3,
        back_scratch
        + [
            DMA((3,)),
            pltpu.VMEM((snaps_here, items_here, channels), BF16),
            pltpu.VMEM((domains, block, channels), BF16),
        ],
        flops=26 * item_flops,
        moved=20 * items_here * channels * 2,
    )(
        cols,
        hidden_a,
        hidden_b,
        hidden_n,
        cotangent,
        temporal_weight,
        twt,
        temporal_bias.reshape(1, doubled),
        spatial_weight,
        adj_flat,
    )
    partial_n = lax.ppermute(partial, "snap", other_snap)
    back_b = exchange(shares_b)

    results = call(
        functools.partial(inner_body, chips, blocks_here, slots),
        [two] * chips + [local_shape],
        [SMEM] + [VMEM] * 3 + [HBM],
        [VMEM] * (chips + 1),
        back_scratch
        + [pltpu.VMEM((1, items_here * slots, block), BF16), DMA((pl.cdiv(blocks_here, 3),))],
        flops=(slots + 1) * item_flops,
        moved=12 * items_here * channels * 2,
    )(cols, rest_a, partial_n, spatial_weight, in_hbm(adj_flat))
    shares_a, local_a = results[:chips], results[chips]
    back_a = to_chips(shares_a, BACKWARD)
    swapped = swap_cores(
        call(
            functools.partial(collect_body, [(i, 1) for i in range(chips)]),
            shape((chips, block, channels)),
            [HBM] * chips,
            HBM,
            [DMA((chips,))],
            moved=2 * chips * block_bytes,
        )(shares_a[0], *back_a)
    )

    acc = pltpu.VMEM((blocks_here, block, channels), F32)
    cost = dict(flops=domains * block * channels, moved=8 * items_here * channels * 2)
    grad_b = call(
        functools.partial(final_outer_body, domains),
        shape((items_here, channels)),
        [SMEM] + [VMEM] * 2,
        VMEM,
        [acc],
        **cost,
    )(send_lists, local_b, back_b)
    part = call(
        functools.partial(final_inner_body, chips),
        local_shape,
        [SMEM] + [VMEM] * chips,
        VMEM,
        **cost,
    )(send_lists, local_a, *back_a)
    input_grad = call(
        functools.partial(last_body, chips),
        shape_hbm((snaps_here, items_here, channels)),
        [SMEM] + [VMEM] * 3,
        HBM,
        [acc, pltpu.VMEM((items_here, channels), BF16), DMA((blocks_here + 1,))],
        **cost,
    )(send_lists, part, swapped, grad_b)
    return output, input_grad


def pad_time(values):
    return jnp.pad(values, ((1, 1), (0, 0), (0, 0)))


def to_items(values):
    return lax.all_to_all(values, "snap", split_axis=1, concat_axis=0, tiled=True)


def to_snaps(values):
    return lax.all_to_all(values, "snap", split_axis=0, concat_axis=1, tiled=True)


def gate_terms(padded, temporal_weight, temporal_bias):
    length = padded.shape[0] - 2
    row_count = padded.shape[1]
    channels = padded.shape[2]
    running = jnp.zeros((length * row_count, temporal_weight.shape[2]), jnp.float32)
    for offset in range(temporal_weight.shape[0]):
        window = padded[offset : offset + length].reshape(length * row_count, channels)
        running = running + jnp.dot(
            window, temporal_weight[offset], preferred_element_type=jnp.float32
        )
    return (running + temporal_bias).reshape(length, row_count, -1)


def gate_forward(mixture, channels):
    linear = mixture[..., :channels]
    gate_value = jax.nn.sigmoid(mixture[..., channels:])
    return ((linear * gate_value).astype(jnp.bfloat16), linear, gate_value)


def gate_backward(upstream, linear, gate_value):
    upstream_f = upstream.astype(jnp.float32)
    return jnp.concatenate(
        [upstream_f * gate_value, upstream_f * linear * gate_value * (1.0 - gate_value)], axis=-1
    ).astype(jnp.bfloat16)


def spread_back(padded_grad, temporal_weight):
    length = padded_grad.shape[0] - 2
    row_count = padded_grad.shape[1]
    doubled = padded_grad.shape[2]
    channels = temporal_weight.shape[1]
    taps_count = temporal_weight.shape[0]
    running = jnp.zeros((length * row_count, channels), jnp.float32)
    for offset in range(taps_count):
        start = taps_count - 1 - offset
        window = padded_grad[start : start + length].reshape(length * row_count, doubled)
        running = running + lax.dot_general(
            window,
            temporal_weight[offset],
            (((1,), (1,)), ((), ())),
            preferred_element_type=jnp.float32,
        )
    return running.reshape(length, row_count, channels).astype(jnp.bfloat16)


def local_any(
    features,
    adjacency,
    block_cols,
    send_lists,
    receive_lists,
    spatial_weight,
    temporal_weight,
    temporal_bias,
    cotangent,
):
    domains = lax.axis_size("dom")
    snaps_here, items_here, channels = features.shape
    slot_count = adjacency.shape[2]
    block_size = adjacency.shape[3]
    blocks_here = items_here // block_size
    frame_size = blocks_here + domains
    own_blocks = features.reshape(snaps_here, blocks_here, block_size, channels)
    adjacency_tiles = adjacency.reshape(snaps_here, blocks_here, block_size, slot_count, block_size)
    wanted = send_lists[:, 0, :]
    selector = (wanted[:, :, None] == jnp.arange(blocks_here)[None, None, :]).astype(jnp.bfloat16)
    outgoing = jnp.einsum(
        "sqn,snbc->sqbc", selector, own_blocks, preferred_element_type=jnp.float32
    ).astype(jnp.bfloat16)
    arrived = lax.all_to_all(outgoing, "dom", split_axis=1, concat_axis=1, tiled=True)
    snap_rows = jnp.arange(snaps_here)[:, None, None]
    extended = jnp.concatenate([own_blocks, arrived], axis=1)
    neighbours = extended[snap_rows, block_cols]
    aggregated = jnp.einsum(
        "sjrkc,sjkcd->sjrd", adjacency_tiles, neighbours, preferred_element_type=jnp.float32
    )
    aggregated = aggregated.astype(jnp.bfloat16).reshape(snaps_here * items_here, channels)
    hidden = jnp.dot(aggregated, spatial_weight, preferred_element_type=jnp.float32).astype(
        jnp.bfloat16
    )
    hidden = hidden.reshape(snaps_here, items_here, channels)
    hidden_items = to_items(hidden)
    mixture = gate_terms(pad_time(hidden_items), temporal_weight, temporal_bias)
    output_items, linear, gate_value = gate_forward(mixture, channels)
    output = to_snaps(output_items)
    gate_grad = gate_backward(to_items(cotangent), linear, gate_value)
    hidden_grad = to_snaps(spread_back(pad_time(gate_grad), temporal_weight))
    aggregate_grad = lax.dot_general(
        hidden_grad.reshape(snaps_here * items_here, channels),
        spatial_weight,
        (((1,), (1,)), ((), ())),
        preferred_element_type=jnp.float32,
    ).astype(jnp.bfloat16)
    aggregate_grad = aggregate_grad.reshape(snaps_here, blocks_here, block_size, channels)
    contribution = jnp.einsum(
        "sjrkc,sjrd->sjkcd", adjacency_tiles, aggregate_grad, preferred_element_type=jnp.float32
    )
    placing = (block_cols[..., None] == jnp.arange(frame_size)[None, None, None, :]).astype(
        jnp.float32
    )
    framed = jnp.einsum(
        "sjkf,sjkcd->sfcd",
        placing,
        contribution,
        precision=lax.Precision.HIGHEST,
        preferred_element_type=jnp.float32,
    )
    returned = lax.all_to_all(
        framed[:, blocks_here:].astype(jnp.bfloat16), "dom", split_axis=1, concat_axis=1, tiled=True
    )
    input_grad = framed[:, :blocks_here] + jnp.einsum(
        "sqn,sqbc->snbc", selector, returned, preferred_element_type=jnp.float32
    )
    return (output, input_grad.reshape(snaps_here, items_here, channels).astype(jnp.bfloat16))


def solution(mesh):
    paired = mesh.shape["snap"] == 2 and mesh.shape["dom"] == 16
    return jax.shard_map(
        local_pair if paired else local_any,
        mesh=mesh,
        in_specs=(
            P("snap", "dom", None),
            P("snap", "dom", None, None),
            P("snap", "dom", None),
            P("snap", "dom", None),
            P("snap", "dom", None),
            P(),
            P(),
            P(),
            P("snap", "dom", None),
        ),
        out_specs=(P("snap", "dom", None), P("snap", "dom", None)),
        check_vma=False,
    )
```

```python
import functools

import jax
import jax.numpy as jnp
from jax import lax
from jax.experimental import pallas as pl
from jax.experimental.pallas import tpu as pltpu
from jax.sharding import PartitionSpec as P

F32 = jnp.float32
BF16 = jnp.bfloat16
VMEM = pl.BlockSpec(memory_space=pltpu.VMEM)
SMEM = pl.BlockSpec(memory_space=pltpu.SMEM)
HBM = pl.BlockSpec(memory_space=pltpu.MemorySpace.HBM)
TILE = 384
VMEM_LIMIT = 16 * 1024 * 1024
DMA = pltpu.SemaphoreType.DMA
FORWARD = (1, 3, 2, 5, 4, 7, 6)
BACKWARD = (1, 2, 3, 5, 4, 7, 6)
COST = 100


def dot(a, b):
    return jnp.dot(a, b, preferred_element_type=F32)


def dot_t(a, b):
    return lax.dot_general(a, b, (((1,), (1,)), ((), ())), preferred_element_type=F32)


def shape(dims, dtype=BF16):
    return jax.ShapeDtypeStruct(dims, dtype)


def shape_hbm(dims, dtype=BF16):
    return pltpu.MemorySpace.HBM(dims, dtype)


def in_hbm(values):
    return pltpu.with_memory_space_constraint(values, pltpu.MemorySpace.HBM)


def call(body, outs, in_specs, out_specs, scratch=(), flops=0, moved=0):
    return pl.pallas_call(
        body,
        out_shape=outs,
        in_specs=in_specs,
        out_specs=out_specs,
        scratch_shapes=list(scratch),
        compiler_params=pltpu.CompilerParams(vmem_limit_bytes=VMEM_LIMIT),
        cost_estimate=pl.CostEstimate(flops=COST * flops, bytes_accessed=COST * moved, transcendentals=0),
    )


def inner_index():
    return 1 - lax.axis_index("snap")


def split_index():
    me = lax.axis_index("dom")
    return me // 2, lax.rem(me, 2)


def run_copies(pairs, sem):
    copies = [
        pltpu.make_async_copy(source, target, sem.at[i]) for i, (source, target) in enumerate(pairs)
    ]
    for copy in copies:
        copy.start()
    for copy in copies:
        copy.wait()


def wanted(lists, feats, snap, target, block):
    start = pl.multiple_of(jnp.maximum(lists[snap, 0, target], 0) * block, block)
    return feats.at[pl.ds(start, block)]


def pack_inner_body(domains, block, lists, feats, out, held, send, sem):
    ia = inner_index()
    run_copies([(lists, send), (feats.at[ia], held)], sem)
    pairs = [(wanted(send, held, ia, d, block), out.at[d]) for d in range(domains)]
    run_copies(pairs, sem)


def pack_outer_body(chips, block, lists, partner_lists, feats, partner_feats, *rest):
    outs, (held, partner_held, send, partner_send, sem) = rest[:-5], rest[-5:]
    chip, core = split_index()
    ib = 1 - inner_index()
    run_copies(
        [
            (lists, send),
            (partner_lists, partner_send),
            (feats.at[ib], held),
            (partner_feats.at[ib], partner_held),
        ],
        sem,
    )
    for offset in range(1, chips):
        target = 2 * jnp.bitwise_xor(chip, offset) + core
        outs[offset - 1][0] = wanted(send, held, ib, target, block)[...]
        outs[offset - 1][1] = wanted(partner_send, partner_held, ib, target, block)[...]


def collect_body(picks, *refs):
    sources, out, sem = refs[:-2], refs[-2], refs[-1]
    run_copies([(sources[i].at[j], out.at[n]) for n, (i, j) in enumerate(picks)], sem)


def turn_body(tw, twt):
    for tap in range(tw.shape[0]):
        twt[tap] = tw[tap].astype(F32).T.astype(BF16)


def position(column, chips, blocks_here, plain):
    chip, core = split_index()
    part = jnp.clip(column - blocks_here, 0, 2 * chips - 1)
    if plain:
        return part
    which = jnp.bitwise_xor(lax.rem(part, 2), core)
    return which * chips + jnp.bitwise_xor(part // 2, chip)


def side_by_side(snap, slots, adj, wide, tiles, fetches=()):
    blocks_here, block = tiles.shape[:2]
    rows = slots * block
    for j in range(blocks_here):
        if fetches and j % 3 == 0:
            fetches[j // 3].wait()
        wide[j % 2] = adj[snap, j * rows : (j + 1) * rows, :].astype(F32)
        for slot in range(slots):
            tile = wide[j % 2, pl.ds(slot, block, stride=slots), :]
            tiles[j, :, slot * block : (slot + 1) * block] = tile.astype(BF16)


def aggregate(plain, snap, chips, slots, cols, own, tiles, halo, agg, sw, hidden):
    blocks_here, block = tiles.shape[:2]
    for j in range(blocks_here):
        rows = slice(j * block, (j + 1) * block)
        pieces = [own[rows, :]]
        for slot in range(1, slots):
            pieces.append(halo[position(cols[snap, slot, j], chips, blocks_here, plain)])
        agg[rows, :] = dot(tiles[j], jnp.concatenate(pieces, axis=0)).astype(BF16)
    hidden[...] = dot(agg[...], sw[...]).astype(BF16)


def hidden_body(inner, chips, slots, cols, feats, adj, weight, *rest):
    arrived, rest = rest[:-8], rest[-8:]
    hidden, own, sw, wide, tiles, halo, agg, sem = rest
    snap = inner_index() if inner else 1 - inner_index()
    pairs = [(feats.at[snap], own), (weight, sw)]
    if inner:
        pairs.append((arrived[0], halo))
    else:
        lists, partner_feats, arrived = arrived[0], arrived[1], arrived[2:]
        me = lax.axis_index("dom")
        block = halo.shape[1]
        pairs.append((wanted(lists, partner_feats.at[snap], snap, me, block), halo.at[chips]))
        for offset, source in zip(FORWARD, arrived):
            for which in range(2):
                pairs.append((source.at[which], halo.at[which * chips + offset]))
    copies = [
        pltpu.make_async_copy(source, target, sem.at[i]) for i, (source, target) in enumerate(pairs)
    ]
    for copy in copies:
        copy.start()
    side_by_side(snap, slots, adj, wide, tiles)
    for copy in copies:
        copy.wait()
    aggregate(inner, snap, chips, slots, cols, own, tiles, halo, agg, sw, hidden)


def spread(plain, snap, chips, blocks_here, slots, cols, grad, sw, adj, local, acc):
    block = acc.shape[1]
    agg_t = dot_t(sw[...], grad[...]).astype(BF16)
    acc[...] = jnp.zeros_like(acc)
    for j in range(blocks_here):
        parts = dot(agg_t[:, j * block : (j + 1) * block], adj[j])
        local[j] = parts[:, :block]
        for slot in range(1, slots):
            at = position(cols[snap, slot, j], chips, blocks_here, plain)
            acc[at] = acc[at] + parts[:, slot * block : (slot + 1) * block]


def temporal_body(
    chips, blocks_here, slots, tile, cols, ha, hb, hn, cot, tw, twt, bias, sw, raw, *rest
):
    shares, out, partial, rest_a, local, grad, acc, adj, wide, sem, held, held_shares = rest
    ia = inner_index()
    ib = 1 - ia
    flip = lax.axis_index("snap")
    lo, hi = 2 * flip, 2 - 2 * flip
    items, channels = ha.shape
    both = jnp.concatenate(
        [
            jnp.concatenate([tw[lo], tw[1]], axis=0),
            jnp.concatenate([tw[1], tw[hi]], axis=0),
        ],
        axis=1,
    )
    back = jnp.concatenate([twt[hi], twt[1]], axis=1)
    for start in range(0, items, tile):
        rows = slice(start, start + tile)
        pair = jnp.concatenate([hb[rows, :], ha[rows, :]], axis=1)
        mixes = dot(pair, both)
        mix_a = mixes[:, : 2 * channels] + dot(hn[rows, :], tw[hi]) + bias[...]
        mix_b = mixes[:, 2 * channels :] + bias[...]
        grads = []
        for index, mix in ((ia, mix_a), (ib, mix_b)):
            linear = mix[:, :channels]
            gate = 0.5 * jnp.tanh(0.5 * mix[:, channels:]) + 0.5
            up = cot[index, rows, :].astype(F32)
            gated = linear * gate
            held[index, rows, :] = gated.astype(BF16)
            first = up * gate
            second = up * gated * (1.0 - gate)
            grads.append(jnp.concatenate([first.astype(BF16), second.astype(BF16)], axis=1))
        ga, gb = grads
        from_a = dot(ga, back)
        from_b = dot(gb, back)
        partial[rows, :] = from_a[:, :channels].astype(BF16)
        rest_a[rows, :] = from_a[:, channels:] + from_b[:, :channels]
        grad[rows, :] = (dot(ga, twt[lo]) + from_b[:, channels:]).astype(BF16)
    emit = pltpu.make_async_copy(held, out, sem.at[2])
    emit.start()
    side_by_side(ib, slots, raw, wide, adj)
    spread(True, ib, chips, blocks_here, slots, cols, grad, sw, adj, local, acc)
    half = acc.shape[0] // 2
    copies = [emit]
    for n in range(2):
        some = pl.ds(n * half, half)
        held_shares[some] = acc[some].astype(BF16)
        copies.append(pltpu.make_async_copy(held_shares.at[some], shares.at[some], sem.at[n]))
        copies[-1].start()
    for copy in copies:
        copy.wait()


def inner_body(chips, blocks_here, slots, cols, rest_a, partial, sw, raw, *rest):
    outs = rest[:chips]
    local, grad, acc, adj, wide, held, sem = rest[chips:]
    ia = inner_index()
    rows = held.shape[1] // blocks_here
    fetches = []
    for j in range(0, blocks_here, 3):
        some = pl.ds(j * rows, min(3, blocks_here - j) * rows)
        fetches.append(
            pltpu.make_async_copy(raw.at[ia, some], held.at[0, some], sem.at[len(fetches)])
        )
        fetches[-1].start()
    grad[...] = (rest_a[...] + partial[...].astype(F32)).astype(BF16)
    side_by_side(0, slots, held, wide, adj, fetches)
    spread(False, ia, chips, blocks_here, slots, cols, grad, sw, adj, local, acc)
    for offset in range(chips):
        for which in range(2):
            outs[offset][which] = acc[which * chips + offset].astype(BF16)


def add_shares(snap, send, local, terms, acc):
    acc[...] = local[...]
    for source, value in terms:
        at = send[snap, 0, source]

        @pl.when(at >= 0)
        def _():
            acc[at] = acc[at] + value[...].astype(F32)


def finish_rows(acc, n):
    return acc[n].T.astype(BF16)


def source_of(offset, which):
    chip, core = split_index()
    return 2 * jnp.bitwise_xor(chip, offset) + jnp.bitwise_xor(core, which)


def final_outer_body(domains, send, local, arrived, out, acc):
    terms = [(d, arrived.at[d]) for d in range(domains)]
    add_shares(1 - inner_index(), send, local, terms, acc)
    block = acc.shape[1]
    for n in range(acc.shape[0]):
        out[n * block : (n + 1) * block, :] = finish_rows(acc, n)


def final_inner_body(chips, send, local, *rest):
    arrived, acc = rest[: chips - 1], rest[chips - 1]
    terms = [(source_of(offset, 0), value.at[0]) for offset, value in zip(BACKWARD, arrived)]
    add_shares(inner_index(), send, local, terms, acc)


def last_body(chips, send, part, swapped, outer, out, acc, held, sem):
    ia = inner_index()
    copies = [pltpu.make_async_copy(outer, out.at[1 - ia], sem.at[0])]
    copies[0].start()
    terms = [(source_of(o, 1), swapped.at[n]) for n, o in enumerate((0,) + BACKWARD)]
    add_shares(ia, send, part, terms, acc)
    block = acc.shape[1]
    for n in range(acc.shape[0]):
        rows = pl.ds(n * block, block)
        held[rows, :] = finish_rows(acc, n)
        copies.append(pltpu.make_async_copy(held.at[rows], out.at[ia, rows], sem.at[n + 1]))
        copies[-1].start()
    for copy in copies:
        copy.wait()


def local_pair(
    features,
    adjacency,
    block_cols,
    send_lists,
    receive_lists,
    spatial_weight,
    temporal_weight,
    temporal_bias,
    cotangent,
):
    domains = lax.axis_size("dom")
    chips = domains // 2
    snaps_here, items_here, channels = features.shape
    slots, block = adjacency.shape[2:]
    blocks_here = items_here // block
    taps, _, doubled = temporal_weight.shape
    flip_core = [(i, i ^ 1) for i in range(domains)]
    other_snap = [(0, 1), (1, 0)]
    two = shape((2, block, channels))
    block_bytes = block * channels * 2
    item_flops = 2 * items_here * channels * channels

    def swap_cores(values):
        return lax.ppermute(values, "dom", flip_core)

    def exchange(values):
        return lax.all_to_all(values, "dom", split_axis=0, concat_axis=0, tiled=True)

    def to_chips(payloads, order):
        done = {}
        for offset in order:
            pairs = [(i, i ^ (2 * offset)) for i in range(domains)]
            done[offset] = lax.ppermute(payloads[offset], "dom", pairs)
        return [done[offset] for offset in order]

    cols = jnp.swapaxes(block_cols, 1, 2)
    partner_send = swap_cores(send_lists)
    partner_feats = swap_cores(features)

    packed_a = call(
        functools.partial(pack_inner_body, domains, block),
        shape_hbm((domains, block, channels)),
        [HBM] * 2,
        HBM,
        [
            pltpu.VMEM((items_here, channels), BF16),
            pltpu.SMEM(send_lists.shape, jnp.int32),
            DMA((domains,)),
        ],
        moved=2 * domains * block_bytes,
    )(in_hbm(send_lists), in_hbm(features))
    packed_a, partner_send, partner_feats = lax.optimization_barrier(
        (packed_a, partner_send, partner_feats)
    )
    got_a = exchange(packed_a)
    packed = call(
        functools.partial(pack_outer_body, chips, block),
        [two] * (chips - 1),
        [HBM] * 4,
        [VMEM] * (chips - 1),
        [
            pltpu.VMEM((items_here, channels), BF16),
            pltpu.VMEM((items_here, channels), BF16),
            pltpu.SMEM(send_lists.shape, jnp.int32),
            pltpu.SMEM(send_lists.shape, jnp.int32),
            DMA((4,)),
        ],
        moved=2 * domains * block_bytes,
    )(*(in_hbm(v) for v in (send_lists, partner_send, features, partner_feats)))
    got_b = to_chips(dict(zip(range(1, chips), packed)), FORWARD)

    tile_rows = block * slots
    adj_flat = adjacency.reshape(snaps_here, items_here * slots, block)
    twt = call(
        turn_body,
        shape((taps, doubled, channels)),
        [VMEM],
        VMEM,
        moved=4 * taps * channels * doubled,
    )(temporal_weight)

    def hidden_of(inner, arrived, extra=()):
        return call(
            functools.partial(hidden_body, inner, chips, slots),
            shape((items_here, channels)),
            [SMEM, HBM, VMEM, HBM] + [SMEM, HBM][: len(extra)] + [HBM] * len(arrived),
            VMEM,
            [
                pltpu.VMEM((items_here, channels), BF16),
                pltpu.VMEM((channels, channels), BF16),
                pltpu.VMEM((2, tile_rows, block), F32),
                pltpu.VMEM((blocks_here, block, tile_rows), BF16),
                pltpu.VMEM((domains, block, channels), BF16),
                pltpu.VMEM((items_here, channels), BF16),
                DMA((domains + 2,)),
            ],
            flops=(slots + 1) * item_flops,
            moved=(slots + 4) * items_here * channels * 2,
        )(cols, features, adj_flat, in_hbm(spatial_weight), *extra, *(in_hbm(v) for v in arrived))

    hidden_a = hidden_of(True, [got_a])
    hidden_n = lax.ppermute(hidden_a, "snap", other_snap)
    hidden_b = hidden_of(False, got_b, (partner_send, in_hbm(partner_feats)))

    back_scratch = [
        pltpu.VMEM((items_here, channels), BF16),
        pltpu.VMEM((domains, block, channels), F32),
        pltpu.VMEM((blocks_here, block, tile_rows), BF16),
        pltpu.VMEM((2, tile_rows, block), F32),
    ]
    local_shape = shape((blocks_here, block, channels), F32)
    shares_b, output, partial, rest_a, local_b = call(
        functools.partial(temporal_body, chips, blocks_here, slots, TILE),
        [
            shape_hbm((domains, block, channels)),
            shape_hbm((snaps_here, items_here, channels)),
            shape((items_here, channels)),
            shape((items_here, channels), F32),
            local_shape,
        ],
        [SMEM] + [VMEM] * 9,
        [HBM] * 2 + [VMEM] * 3,
        back_scratch
        + [
            DMA((3,)),
            pltpu.VMEM((snaps_here, items_here, channels), BF16),
            pltpu.VMEM((domains, block, channels), BF16),
        ],
        flops=26 * item_flops,
        moved=20 * items_here * channels * 2,
    )(
        cols,
        hidden_a,
        hidden_b,
        hidden_n,
        cotangent,
        temporal_weight,
        twt,
        temporal_bias.reshape(1, doubled),
        spatial_weight,
        adj_flat,
    )
    partial_n = lax.ppermute(partial, "snap", other_snap)
    back_b = exchange(shares_b)

    results = call(
        functools.partial(inner_body, chips, blocks_here, slots),
        [two] * chips + [local_shape],
        [SMEM] + [VMEM] * 3 + [HBM],
        [VMEM] * (chips + 1),
        back_scratch
        + [pltpu.VMEM((1, items_here * slots, block), BF16), DMA((pl.cdiv(blocks_here, 3),))],
        flops=(slots + 1) * item_flops,
        moved=12 * items_here * channels * 2,
    )(cols, rest_a, partial_n, spatial_weight, in_hbm(adj_flat))
    shares_a, local_a = results[:chips], results[chips]
    back_a = to_chips(shares_a, BACKWARD)
    swapped = swap_cores(
        call(
            functools.partial(collect_body, [(i, 1) for i in range(chips)]),
            shape((chips, block, channels)),
            [HBM] * chips,
            HBM,
            [DMA((chips,))],
            moved=2 * chips * block_bytes,
        )(shares_a[0], *back_a)
    )

    acc = pltpu.VMEM((blocks_here, block, channels), F32)
    cost = dict(flops=domains * block * channels, moved=8 * items_here * channels * 2)
    grad_b = call(
        functools.partial(final_outer_body, domains),
        shape((items_here, channels)),
        [SMEM] + [VMEM] * 2,
        VMEM,
        [acc],
        **cost,
    )(send_lists, local_b, back_b)
    part = call(
        functools.partial(final_inner_body, chips),
        local_shape,
        [SMEM] + [VMEM] * chips,
        VMEM,
        **cost,
    )(send_lists, local_a, *back_a)
    input_grad = call(
        functools.partial(last_body, chips),
        shape_hbm((snaps_here, items_here, channels)),
        [SMEM] + [VMEM] * 3,
        HBM,
        [acc, pltpu.VMEM((items_here, channels), BF16), DMA((blocks_here + 1,))],
        **cost,
    )(send_lists, part, swapped, grad_b)
    return output, input_grad


def pad_time(values):
    return jnp.pad(values, ((1, 1), (0, 0), (0, 0)))


def to_items(values):
    return lax.all_to_all(values, "snap", split_axis=1, concat_axis=0, tiled=True)


def to_snaps(values):
    return lax.all_to_all(values, "snap", split_axis=0, concat_axis=1, tiled=True)


def gate_terms(padded, temporal_weight, temporal_bias):
    length = padded.shape[0] - 2
    row_count = padded.shape[1]
    channels = padded.shape[2]
    running = jnp.zeros((length * row_count, temporal_weight.shape[2]), jnp.float32)
    for offset in range(temporal_weight.shape[0]):
        window = padded[offset : offset + length].reshape(length * row_count, channels)
        running = running + jnp.dot(
            window, temporal_weight[offset], preferred_element_type=jnp.float32
        )
    return (running + temporal_bias).reshape(length, row_count, -1)


def gate_forward(mixture, channels):
    linear = mixture[..., :channels]
    gate_value = jax.nn.sigmoid(mixture[..., channels:])
    return ((linear * gate_value).astype(jnp.bfloat16), linear, gate_value)


def gate_backward(upstream, linear, gate_value):
    upstream_f = upstream.astype(jnp.float32)
    return jnp.concatenate(
        [upstream_f * gate_value, upstream_f * linear * gate_value * (1.0 - gate_value)], axis=-1
    ).astype(jnp.bfloat16)


def spread_back(padded_grad, temporal_weight):
    length = padded_grad.shape[0] - 2
    row_count = padded_grad.shape[1]
    doubled = padded_grad.shape[2]
    channels = temporal_weight.shape[1]
    taps_count = temporal_weight.shape[0]
    running = jnp.zeros((length * row_count, channels), jnp.float32)
    for offset in range(taps_count):
        start = taps_count - 1 - offset
        window = padded_grad[start : start + length].reshape(length * row_count, doubled)
        running = running + lax.dot_general(
            window,
            temporal_weight[offset],
            (((1,), (1,)), ((), ())),
            preferred_element_type=jnp.float32,
        )
    return running.reshape(length, row_count, channels).astype(jnp.bfloat16)


def local_any(
    features,
    adjacency,
    block_cols,
    send_lists,
    receive_lists,
    spatial_weight,
    temporal_weight,
    temporal_bias,
    cotangent,
):
    domains = lax.axis_size("dom")
    snaps_here, items_here, channels = features.shape
    slot_count = adjacency.shape[2]
    block_size = adjacency.shape[3]
    blocks_here = items_here // block_size
    frame_size = blocks_here + domains
    own_blocks = features.reshape(snaps_here, blocks_here, block_size, channels)
    adjacency_tiles = adjacency.reshape(snaps_here, blocks_here, block_size, slot_count, block_size)
    wanted = send_lists[:, 0, :]
    selector = (wanted[:, :, None] == jnp.arange(blocks_here)[None, None, :]).astype(jnp.bfloat16)
    outgoing = jnp.einsum(
        "sqn,snbc->sqbc", selector, own_blocks, preferred_element_type=jnp.float32
    ).astype(jnp.bfloat16)
    arrived = lax.all_to_all(outgoing, "dom", split_axis=1, concat_axis=1, tiled=True)
    snap_rows = jnp.arange(snaps_here)[:, None, None]
    extended = jnp.concatenate([own_blocks, arrived], axis=1)
    neighbours = extended[snap_rows, block_cols]
    aggregated = jnp.einsum(
        "sjrkc,sjkcd->sjrd", adjacency_tiles, neighbours, preferred_element_type=jnp.float32
    )
    aggregated = aggregated.astype(jnp.bfloat16).reshape(snaps_here * items_here, channels)
    hidden = jnp.dot(aggregated, spatial_weight, preferred_element_type=jnp.float32).astype(
        jnp.bfloat16
    )
    hidden = hidden.reshape(snaps_here, items_here, channels)
    hidden_items = to_items(hidden)
    mixture = gate_terms(pad_time(hidden_items), temporal_weight, temporal_bias)
    output_items, linear, gate_value = gate_forward(mixture, channels)
    output = to_snaps(output_items)
    gate_grad = gate_backward(to_items(cotangent), linear, gate_value)
    hidden_grad = to_snaps(spread_back(pad_time(gate_grad), temporal_weight))
    aggregate_grad = lax.dot_general(
        hidden_grad.reshape(snaps_here * items_here, channels),
        spatial_weight,
        (((1,), (1,)), ((), ())),
        preferred_element_type=jnp.float32,
    ).astype(jnp.bfloat16)
    aggregate_grad = aggregate_grad.reshape(snaps_here, blocks_here, block_size, channels)
    contribution = jnp.einsum(
        "sjrkc,sjrd->sjkcd", adjacency_tiles, aggregate_grad, preferred_element_type=jnp.float32
    )
    placing = (block_cols[..., None] == jnp.arange(frame_size)[None, None, None, :]).astype(
        jnp.float32
    )
    framed = jnp.einsum(
        "sjkf,sjkcd->sfcd",
        placing,
        contribution,
        precision=lax.Precision.HIGHEST,
        preferred_element_type=jnp.float32,
    )
    returned = lax.all_to_all(
        framed[:, blocks_here:].astype(jnp.bfloat16), "dom", split_axis=1, concat_axis=1, tiled=True
    )
    input_grad = framed[:, :blocks_here] + jnp.einsum(
        "sqn,sqbc->snbc", selector, returned, preferred_element_type=jnp.float32
    )
    return (output, input_grad.reshape(snaps_here, items_here, channels).astype(jnp.bfloat16))


def solution(mesh):
    paired = mesh.shape["snap"] == 2 and mesh.shape["dom"] == 16
    return jax.shard_map(
        local_pair if paired else local_any,
        mesh=mesh,
        in_specs=(
            P("snap", "dom", None),
            P("snap", "dom", None, None),
            P("snap", "dom", None),
            P("snap", "dom", None),
            P("snap", "dom", None),
            P(),
            P(),
            P(),
            P("snap", "dom", None),
        ),
        out_specs=(P("snap", "dom", None), P("snap", "dom", None)),
        check_vma=False,
    )
```

```python
import functools

import jax
import jax.numpy as jnp
from jax import lax
from jax.experimental import pallas as pl
from jax.experimental.pallas import tpu as pltpu
from jax.sharding import PartitionSpec as P

F32 = jnp.float32
BF16 = jnp.bfloat16
VMEM = pl.BlockSpec(memory_space=pltpu.VMEM)
SMEM = pl.BlockSpec(memory_space=pltpu.SMEM)
HBM = pl.BlockSpec(memory_space=pltpu.MemorySpace.HBM)
TILE = 1152
VMEM_LIMIT = 16 * 1024 * 1024
DMA = pltpu.SemaphoreType.DMA
FORWARD = (1, 3, 2, 5, 4, 7, 6)
BACKWARD = (1, 2, 3, 5, 4, 7, 6)
COST = 100


def dot(a, b):
    return jnp.dot(a, b, preferred_element_type=F32)


def dot_t(a, b):
    return lax.dot_general(a, b, (((1,), (1,)), ((), ())), preferred_element_type=F32)


def shape(dims, dtype=BF16):
    return jax.ShapeDtypeStruct(dims, dtype)


def shape_hbm(dims, dtype=BF16):
    return pltpu.MemorySpace.HBM(dims, dtype)


def in_hbm(values):
    return pltpu.with_memory_space_constraint(values, pltpu.MemorySpace.HBM)


def call(body, outs, in_specs, out_specs, scratch=(), flops=0, moved=0):
    return pl.pallas_call(
        body,
        out_shape=outs,
        in_specs=in_specs,
        out_specs=out_specs,
        scratch_shapes=list(scratch),
        compiler_params=pltpu.CompilerParams(vmem_limit_bytes=VMEM_LIMIT),
        cost_estimate=pl.CostEstimate(flops=COST * flops, bytes_accessed=COST * moved, transcendentals=0),
    )


def inner_index():
    return 1 - lax.axis_index("snap")


def split_index():
    me = lax.axis_index("dom")
    return me // 2, lax.rem(me, 2)


def run_copies(pairs, sem):
    copies = [
        pltpu.make_async_copy(source, target, sem.at[i]) for i, (source, target) in enumerate(pairs)
    ]
    for copy in copies:
        copy.start()
    for copy in copies:
        copy.wait()


def wanted(lists, feats, snap, target, block):
    start = pl.multiple_of(jnp.maximum(lists[snap, 0, target], 0) * block, block)
    return feats.at[pl.ds(start, block)]


def pack_inner_body(domains, block, lists, feats, out, held, send, sem):
    ia = inner_index()
    run_copies([(lists, send), (feats.at[ia], held)], sem)
    pairs = [(wanted(send, held, ia, d, block), out.at[d]) for d in range(domains)]
    run_copies(pairs, sem)


def pack_outer_body(chips, block, lists, partner_lists, feats, partner_feats, *rest):
    outs, (held, partner_held, send, partner_send, sem) = rest[:-5], rest[-5:]
    chip, core = split_index()
    ib = 1 - inner_index()
    run_copies(
        [
            (lists, send),
            (partner_lists, partner_send),
            (feats.at[ib], held),
            (partner_feats.at[ib], partner_held),
        ],
        sem,
    )
    for offset in range(chips):
        target = 2 * jnp.bitwise_xor(chip, offset) + core
        outs[offset][0] = wanted(send, held, ib, target, block)[...]
        outs[offset][1] = wanted(partner_send, partner_held, ib, target, block)[...]


def collect_body(picks, *refs):
    sources, out, sem = refs[:-2], refs[-2], refs[-1]
    run_copies([(sources[i].at[j], out.at[n]) for n, (i, j) in enumerate(picks)], sem)


def turn_body(tw, twt):
    for tap in range(tw.shape[0]):
        twt[tap] = tw[tap].astype(F32).T.astype(BF16)


def position(column, chips, blocks_here, plain):
    chip, core = split_index()
    part = jnp.clip(column - blocks_here, 0, 2 * chips - 1)
    if plain:
        return part
    which = jnp.bitwise_xor(lax.rem(part, 2), core)
    return which * chips + jnp.bitwise_xor(part // 2, chip)


def side_by_side(snap, slots, adj, wide, tiles, fetches=()):
    blocks_here, block = tiles.shape[:2]
    rows = slots * block
    for j in range(blocks_here):
        if fetches and j % 3 == 0:
            fetches[j // 3].wait()
        wide[j % 2] = adj[snap, j * rows : (j + 1) * rows, :].astype(F32)
        for slot in range(slots):
            tile = wide[j % 2, pl.ds(slot, block, stride=slots), :]
            tiles[j, :, slot * block : (slot + 1) * block] = tile.astype(BF16)


def aggregate(plain, snap, chips, slots, cols, own, tiles, halo, agg, sw, hidden):
    blocks_here, block = tiles.shape[:2]
    for j in range(blocks_here):
        rows = slice(j * block, (j + 1) * block)
        pieces = [own[rows, :]]
        for slot in range(1, slots):
            pieces.append(halo[position(cols[snap, slot, j], chips, blocks_here, plain)])
        agg[rows, :] = dot(tiles[j], jnp.concatenate(pieces, axis=0)).astype(BF16)
    hidden[...] = dot(agg[...], sw[...]).astype(BF16)


def hidden_body(inner, chips, slots, cols, feats, adj, weight, *rest):
    arrived, rest = rest[:-8], rest[-8:]
    hidden, own, sw, wide, tiles, halo, agg, sem = rest
    snap = inner_index() if inner else 1 - inner_index()
    pairs = [(feats.at[snap], own), (weight, sw)]
    if inner:
        pairs.append((arrived[0], halo))
    else:
        for offset, source in zip((0,) + FORWARD, arrived):
            for which in range(2):
                pairs.append((source.at[which], halo.at[which * chips + offset]))
    copies = [
        pltpu.make_async_copy(source, target, sem.at[i]) for i, (source, target) in enumerate(pairs)
    ]
    for copy in copies:
        copy.start()
    side_by_side(snap, slots, adj, wide, tiles)
    for copy in copies:
        copy.wait()
    aggregate(inner, snap, chips, slots, cols, own, tiles, halo, agg, sw, hidden)


def spread(plain, snap, chips, blocks_here, slots, cols, grad, sw, adj, local, acc):
    block = acc.shape[1]
    agg_t = dot_t(sw[...], grad[...]).astype(BF16)
    acc[...] = jnp.zeros_like(acc)
    for j in range(blocks_here):
        parts = dot(agg_t[:, j * block : (j + 1) * block], adj[j])
        local[j] = parts[:, :block]
        for slot in range(1, slots):
            at = position(cols[snap, slot, j], chips, blocks_here, plain)
            acc[at] = acc[at] + parts[:, slot * block : (slot + 1) * block]


def temporal_body(
    chips, blocks_here, slots, tile, cols, ha, hb, hn, cot, tw, twt, bias, sw, raw, *rest
):
    shares, out, partial, rest_a, local, grad, acc, adj, wide, sem, held, held_shares = rest
    ia = inner_index()
    ib = 1 - ia
    flip = lax.axis_index("snap")
    lo, hi = 2 * flip, 2 - 2 * flip
    items, channels = ha.shape
    both = jnp.concatenate(
        [
            jnp.concatenate([tw[lo], tw[1]], axis=0),
            jnp.concatenate([tw[1], tw[hi]], axis=0),
        ],
        axis=1,
    )
    back = jnp.concatenate([twt[hi], twt[1]], axis=1)
    for start in range(0, items, tile):
        rows = slice(start, start + tile)
        pair = jnp.concatenate([hb[rows, :], ha[rows, :]], axis=1)
        mixes = dot(pair, both)
        mix_a = mixes[:, : 2 * channels] + dot(hn[rows, :], tw[hi]) + bias[...]
        mix_b = mixes[:, 2 * channels :] + bias[...]
        grads = []
        for index, mix in ((ia, mix_a), (ib, mix_b)):
            linear = mix[:, :channels]
            gate = jax.nn.sigmoid(mix[:, channels:])
            up = cot[index, rows, :].astype(F32)
            gated = linear * gate
            held[index, rows, :] = gated.astype(BF16)
            first = up * gate
            second = up * gated * (1.0 - gate)
            grads.append(jnp.concatenate([first.astype(BF16), second.astype(BF16)], axis=1))
        ga, gb = grads
        from_a = dot(ga, back)
        from_b = dot(gb, back)
        partial[rows, :] = from_a[:, :channels].astype(BF16)
        rest_a[rows, :] = from_a[:, channels:] + from_b[:, :channels]
        grad[rows, :] = (dot(ga, twt[lo]) + from_b[:, channels:]).astype(BF16)
    emit = pltpu.make_async_copy(held, out, sem.at[2])
    emit.start()
    side_by_side(ib, slots, raw, wide, adj)
    spread(True, ib, chips, blocks_here, slots, cols, grad, sw, adj, local, acc)
    half = acc.shape[0] // 2
    copies = [emit]
    for n in range(2):
        some = pl.ds(n * half, half)
        held_shares[some] = acc[some].astype(BF16)
        copies.append(pltpu.make_async_copy(held_shares.at[some], shares.at[some], sem.at[n]))
        copies[-1].start()
    for copy in copies:
        copy.wait()


def inner_body(chips, blocks_here, slots, cols, rest_a, partial, sw, raw, *rest):
    outs = rest[:chips]
    local, grad, acc, adj, wide, held, sem = rest[chips:]
    ia = inner_index()
    rows = held.shape[1] // blocks_here
    fetches = []
    for j in range(0, blocks_here, 3):
        some = pl.ds(j * rows, min(3, blocks_here - j) * rows)
        fetches.append(
            pltpu.make_async_copy(raw.at[ia, some], held.at[0, some], sem.at[len(fetches)])
        )
        fetches[-1].start()
    grad[...] = (rest_a[...] + partial[...].astype(F32)).astype(BF16)
    side_by_side(0, slots, held, wide, adj, fetches)
    spread(False, ia, chips, blocks_here, slots, cols, grad, sw, adj, local, acc)
    for offset in range(chips):
        for which in range(2):
            outs[offset][which] = acc[which * chips + offset].astype(BF16)


def add_shares(snap, send, local, terms, acc):
    acc[...] = local[...]
    for source, value in terms:
        at = send[snap, 0, source]

        @pl.when(at >= 0)
        def _():
            acc[at] = acc[at] + value[...].astype(F32)


def finish_rows(acc, n):
    return acc[n].T.astype(BF16)


def source_of(offset, which):
    chip, core = split_index()
    return 2 * jnp.bitwise_xor(chip, offset) + jnp.bitwise_xor(core, which)


def final_outer_body(domains, send, local, arrived, out, acc):
    terms = [(d, arrived.at[d]) for d in range(domains)]
    add_shares(1 - inner_index(), send, local, terms, acc)
    block = acc.shape[1]
    for n in range(acc.shape[0]):
        out[n * block : (n + 1) * block, :] = finish_rows(acc, n)


def final_inner_body(chips, send, local, *rest):
    arrived, acc = rest[: chips - 1], rest[chips - 1]
    terms = [(source_of(offset, 0), value.at[0]) for offset, value in zip(BACKWARD, arrived)]
    add_shares(inner_index(), send, local, terms, acc)


def last_body(chips, send, part, swapped, outer, out, acc, held, sem):
    ia = inner_index()
    copies = [pltpu.make_async_copy(outer, out.at[1 - ia], sem.at[0])]
    copies[0].start()
    terms = [(source_of(o, 1), swapped.at[n]) for n, o in enumerate((0,) + BACKWARD)]
    add_shares(ia, send, part, terms, acc)
    block = acc.shape[1]
    for n in range(acc.shape[0]):
        rows = pl.ds(n * block, block)
        held[rows, :] = finish_rows(acc, n)
        copies.append(pltpu.make_async_copy(held.at[rows], out.at[ia, rows], sem.at[n + 1]))
        copies[-1].start()
    for copy in copies:
        copy.wait()


def local_pair(
    features,
    adjacency,
    block_cols,
    send_lists,
    receive_lists,
    spatial_weight,
    temporal_weight,
    temporal_bias,
    cotangent,
):
    domains = lax.axis_size("dom")
    chips = domains // 2
    snaps_here, items_here, channels = features.shape
    slots, block = adjacency.shape[2:]
    blocks_here = items_here // block
    taps, _, doubled = temporal_weight.shape
    flip_core = [(i, i ^ 1) for i in range(domains)]
    other_snap = [(0, 1), (1, 0)]
    two = shape((2, block, channels))
    block_bytes = block * channels * 2
    item_flops = 2 * items_here * channels * channels

    def swap_cores(values):
        return lax.ppermute(values, "dom", flip_core)

    def exchange(values):
        return lax.all_to_all(values, "dom", split_axis=0, concat_axis=0, tiled=True)

    def to_chips(payloads, order):
        done = {}
        for offset in order:
            pairs = [(i, i ^ (2 * offset)) for i in range(domains)]
            done[offset] = lax.ppermute(payloads[offset], "dom", pairs)
        return [done[offset] for offset in order]

    cols = jnp.swapaxes(block_cols, 1, 2)
    partner_send = swap_cores(send_lists)
    partner_feats = swap_cores(features)

    packed_a = call(
        functools.partial(pack_inner_body, domains, block),
        shape_hbm((domains, block, channels)),
        [HBM] * 2,
        HBM,
        [
            pltpu.VMEM((items_here, channels), BF16),
            pltpu.SMEM(send_lists.shape, jnp.int32),
            DMA((domains,)),
        ],
        moved=2 * domains * block_bytes,
    )(in_hbm(send_lists), in_hbm(features))
    packed_a, partner_send, partner_feats = lax.optimization_barrier(
        (packed_a, partner_send, partner_feats)
    )
    got_a = exchange(packed_a)
    packed = call(
        functools.partial(pack_outer_body, chips, block),
        [two] * chips,
        [HBM] * 4,
        [VMEM] * chips,
        [
            pltpu.VMEM((items_here, channels), BF16),
            pltpu.VMEM((items_here, channels), BF16),
            pltpu.SMEM(send_lists.shape, jnp.int32),
            pltpu.SMEM(send_lists.shape, jnp.int32),
            DMA((4,)),
        ],
        moved=2 * domains * block_bytes,
    )(*(in_hbm(v) for v in (send_lists, partner_send, features, partner_feats)))
    got_b = [packed[0]] + to_chips(packed, FORWARD)

    tile_rows = block * slots
    adj_flat = adjacency.reshape(snaps_here, items_here * slots, block)
    twt = call(
        turn_body,
        shape((taps, doubled, channels)),
        [VMEM],
        VMEM,
        moved=4 * taps * channels * doubled,
    )(temporal_weight)

    def hidden_of(inner, arrived):
        return call(
            functools.partial(hidden_body, inner, chips, slots),
            shape((items_here, channels)),
            [SMEM, HBM, VMEM, HBM] + [HBM] * len(arrived),
            VMEM,
            [
                pltpu.VMEM((items_here, channels), BF16),
                pltpu.VMEM((channels, channels), BF16),
                pltpu.VMEM((2, tile_rows, block), F32),
                pltpu.VMEM((blocks_here, block, tile_rows), BF16),
                pltpu.VMEM((domains, block, channels), BF16),
                pltpu.VMEM((items_here, channels), BF16),
                DMA((domains + 2,)),
            ],
            flops=(slots + 1) * item_flops,
            moved=(slots + 4) * items_here * channels * 2,
        )(cols, features, adj_flat, in_hbm(spatial_weight), *(in_hbm(v) for v in arrived))

    hidden_a = hidden_of(True, [got_a])
    hidden_n = lax.ppermute(hidden_a, "snap", other_snap)
    hidden_b = hidden_of(False, got_b)

    back_scratch = [
        pltpu.VMEM((items_here, channels), BF16),
        pltpu.VMEM((domains, block, channels), F32),
        pltpu.VMEM((blocks_here, block, tile_rows), BF16),
        pltpu.VMEM((2, tile_rows, block), F32),
    ]
    local_shape = shape((blocks_here, block, channels), F32)
    shares_b, output, partial, rest_a, local_b = call(
        functools.partial(temporal_body, chips, blocks_here, slots, TILE),
        [
            shape_hbm((domains, block, channels)),
            shape_hbm((snaps_here, items_here, channels)),
            shape((items_here, channels)),
            shape((items_here, channels), F32),
            local_shape,
        ],
        [SMEM] + [VMEM] * 9,
        [HBM] * 2 + [VMEM] * 3,
        back_scratch
        + [
            DMA((3,)),
            pltpu.VMEM((snaps_here, items_here, channels), BF16),
            pltpu.VMEM((domains, block, channels), BF16),
        ],
        flops=26 * item_flops,
        moved=20 * items_here * channels * 2,
    )(
        cols,
        hidden_a,
        hidden_b,
        hidden_n,
        cotangent,
        temporal_weight,
        twt,
        temporal_bias.reshape(1, doubled),
        spatial_weight,
        adj_flat,
    )
    partial_n = lax.ppermute(partial, "snap", other_snap)
    back_b = exchange(shares_b)

    results = call(
        functools.partial(inner_body, chips, blocks_here, slots),
        [two] * chips + [local_shape],
        [SMEM] + [VMEM] * 3 + [HBM],
        [VMEM] * (chips + 1),
        back_scratch
        + [pltpu.VMEM((1, items_here * slots, block), BF16), DMA((pl.cdiv(blocks_here, 3),))],
        flops=(slots + 1) * item_flops,
        moved=12 * items_here * channels * 2,
    )(cols, rest_a, partial_n, spatial_weight, in_hbm(adj_flat))
    shares_a, local_a = results[:chips], results[chips]
    back_a = to_chips(shares_a, BACKWARD)
    swapped = swap_cores(
        call(
            functools.partial(collect_body, [(i, 1) for i in range(chips)]),
            shape((chips, block, channels)),
            [HBM] * chips,
            HBM,
            [DMA((chips,))],
            moved=2 * chips * block_bytes,
        )(shares_a[0], *back_a)
    )

    acc = pltpu.VMEM((blocks_here, block, channels), F32)
    cost = dict(flops=domains * block * channels, moved=8 * items_here * channels * 2)
    grad_b = call(
        functools.partial(final_outer_body, domains),
        shape((items_here, channels)),
        [SMEM] + [VMEM] * 2,
        VMEM,
        [acc],
        **cost,
    )(send_lists, local_b, back_b)
    part = call(
        functools.partial(final_inner_body, chips),
        local_shape,
        [SMEM] + [VMEM] * chips,
        VMEM,
        **cost,
    )(send_lists, local_a, *back_a)
    input_grad = call(
        functools.partial(last_body, chips),
        shape_hbm((snaps_here, items_here, channels)),
        [SMEM] + [VMEM] * 3,
        HBM,
        [acc, pltpu.VMEM((items_here, channels), BF16), DMA((blocks_here + 1,))],
        **cost,
    )(send_lists, part, swapped, grad_b)
    return output, input_grad


def pad_time(values):
    return jnp.pad(values, ((1, 1), (0, 0), (0, 0)))


def to_items(values):
    return lax.all_to_all(values, "snap", split_axis=1, concat_axis=0, tiled=True)


def to_snaps(values):
    return lax.all_to_all(values, "snap", split_axis=0, concat_axis=1, tiled=True)


def gate_terms(padded, temporal_weight, temporal_bias):
    length = padded.shape[0] - 2
    row_count = padded.shape[1]
    channels = padded.shape[2]
    running = jnp.zeros((length * row_count, temporal_weight.shape[2]), jnp.float32)
    for offset in range(temporal_weight.shape[0]):
        window = padded[offset : offset + length].reshape(length * row_count, channels)
        running = running + jnp.dot(
            window, temporal_weight[offset], preferred_element_type=jnp.float32
        )
    return (running + temporal_bias).reshape(length, row_count, -1)


def gate_forward(mixture, channels):
    linear = mixture[..., :channels]
    gate_value = jax.nn.sigmoid(mixture[..., channels:])
    return ((linear * gate_value).astype(jnp.bfloat16), linear, gate_value)


def gate_backward(upstream, linear, gate_value):
    upstream_f = upstream.astype(jnp.float32)
    return jnp.concatenate(
        [upstream_f * gate_value, upstream_f * linear * gate_value * (1.0 - gate_value)], axis=-1
    ).astype(jnp.bfloat16)


def spread_back(padded_grad, temporal_weight):
    length = padded_grad.shape[0] - 2
    row_count = padded_grad.shape[1]
    doubled = padded_grad.shape[2]
    channels = temporal_weight.shape[1]
    taps_count = temporal_weight.shape[0]
    running = jnp.zeros((length * row_count, channels), jnp.float32)
    for offset in range(taps_count):
        start = taps_count - 1 - offset
        window = padded_grad[start : start + length].reshape(length * row_count, doubled)
        running = running + lax.dot_general(
            window,
            temporal_weight[offset],
            (((1,), (1,)), ((), ())),
            preferred_element_type=jnp.float32,
        )
    return running.reshape(length, row_count, channels).astype(jnp.bfloat16)


def local_any(
    features,
    adjacency,
    block_cols,
    send_lists,
    receive_lists,
    spatial_weight,
    temporal_weight,
    temporal_bias,
    cotangent,
):
    domains = lax.axis_size("dom")
    snaps_here, items_here, channels = features.shape
    slot_count = adjacency.shape[2]
    block_size = adjacency.shape[3]
    blocks_here = items_here // block_size
    frame_size = blocks_here + domains
    own_blocks = features.reshape(snaps_here, blocks_here, block_size, channels)
    adjacency_tiles = adjacency.reshape(snaps_here, blocks_here, block_size, slot_count, block_size)
    wanted = send_lists[:, 0, :]
    selector = (wanted[:, :, None] == jnp.arange(blocks_here)[None, None, :]).astype(jnp.bfloat16)
    outgoing = jnp.einsum(
        "sqn,snbc->sqbc", selector, own_blocks, preferred_element_type=jnp.float32
    ).astype(jnp.bfloat16)
    arrived = lax.all_to_all(outgoing, "dom", split_axis=1, concat_axis=1, tiled=True)
    snap_rows = jnp.arange(snaps_here)[:, None, None]
    extended = jnp.concatenate([own_blocks, arrived], axis=1)
    neighbours = extended[snap_rows, block_cols]
    aggregated = jnp.einsum(
        "sjrkc,sjkcd->sjrd", adjacency_tiles, neighbours, preferred_element_type=jnp.float32
    )
    aggregated = aggregated.astype(jnp.bfloat16).reshape(snaps_here * items_here, channels)
    hidden = jnp.dot(aggregated, spatial_weight, preferred_element_type=jnp.float32).astype(
        jnp.bfloat16
    )
    hidden = hidden.reshape(snaps_here, items_here, channels)
    hidden_items = to_items(hidden)
    mixture = gate_terms(pad_time(hidden_items), temporal_weight, temporal_bias)
    output_items, linear, gate_value = gate_forward(mixture, channels)
    output = to_snaps(output_items)
    gate_grad = gate_backward(to_items(cotangent), linear, gate_value)
    hidden_grad = to_snaps(spread_back(pad_time(gate_grad), temporal_weight))
    aggregate_grad = lax.dot_general(
        hidden_grad.reshape(snaps_here * items_here, channels),
        spatial_weight,
        (((1,), (1,)), ((), ())),
        preferred_element_type=jnp.float32,
    ).astype(jnp.bfloat16)
    aggregate_grad = aggregate_grad.reshape(snaps_here, blocks_here, block_size, channels)
    contribution = jnp.einsum(
        "sjrkc,sjrd->sjkcd", adjacency_tiles, aggregate_grad, preferred_element_type=jnp.float32
    )
    placing = (block_cols[..., None] == jnp.arange(frame_size)[None, None, None, :]).astype(
        jnp.float32
    )
    framed = jnp.einsum(
        "sjkf,sjkcd->sfcd",
        placing,
        contribution,
        precision=lax.Precision.HIGHEST,
        preferred_element_type=jnp.float32,
    )
    returned = lax.all_to_all(
        framed[:, blocks_here:].astype(jnp.bfloat16), "dom", split_axis=1, concat_axis=1, tiled=True
    )
    input_grad = framed[:, :blocks_here] + jnp.einsum(
        "sqn,sqbc->snbc", selector, returned, preferred_element_type=jnp.float32
    )
    return (output, input_grad.reshape(snaps_here, items_here, channels).astype(jnp.bfloat16))


def solution(mesh):
    paired = mesh.shape["snap"] == 2 and mesh.shape["dom"] == 16
    return jax.shard_map(
        local_pair if paired else local_any,
        mesh=mesh,
        in_specs=(
            P("snap", "dom", None),
            P("snap", "dom", None, None),
            P("snap", "dom", None),
            P("snap", "dom", None),
            P("snap", "dom", None),
            P(),
            P(),
            P(),
            P("snap", "dom", None),
        ),
        out_specs=(P("snap", "dom", None), P("snap", "dom", None)),
        check_vma=False,
    )
```
